512 devices in a mesh: sub: 8 (over y_lo, core), blk: 64 (over y_hi, x, z).
Axes of the slice: x: 4, y: 8 (y_hi: 2, y_lo: 4; y = y_hi * 4 + y_lo), z: 8, core: 2. Of those that a mesh axis runs over, the one named last changes fastest.
Arguments:
- feats: bfloat16 [8, 2, 4096, 512], P('sub', None, 'blk'), may hold values from -8 to 8
- pos: int32 [8, 4096], P('sub'), may hold values from 0 to 4095, as said below
- w_one: bfloat16 [512, 512], replicated, may hold values from -0.25 to 0.25
- b_one: float32 [512], replicated, may hold values from -3 to 3
- w_two: bfloat16 [512, 512], replicated, may hold values from -0.25 to 0.25
Outputs:
- grad_feats: bfloat16 [8, 2, 4096, 512], P('sub', None, 'blk')
- grad_w_one: float32 [512, 512], P('blk')
- grad_b_one: float32 [512], P('blk')
- grad_w_two: float32 [512, 512], P('blk')
The draws below stay inside these ranges and needn't reach their ends.
Inputs may be any that keep to these rules, and one draw needn't show every extreme that they name: Each row pos[g] names every row of 0 to 4095 exactly once.
All inputs are finite; a program needn't handle non-finite values.
Results may differ from the reference program's by a relative error of at most 0.0059.
Values may be sent and summed in bfloat16 or wider, within the bound.
No kernel may reach another device: no remote copies, remote signals or barrier semaphores. Data moves between devices by JAX's collectives and lax.ppermute only.
A program may use at most 64 MiB of HBM per device.

```python
import math
import jax
import jax.numpy as jnp
from jax import lax

D = 512
NODES = 4096
SUBS = 8


def shared_order(key):
    key_list = jax.random.split(jax.random.fold_in(key, 7001), SUBS)
    return jax.vmap(lambda one_key: jax.random.permutation(one_key, NODES))(key_list).astype(jnp.int32)


def draw_pos(key, part):
    return shared_order(key)


def draw_feats(key, part):
    permuted = shared_order(key)
    key_proto, key_mix, key_augment, key_noise, key_scale = jax.random.split(jax.random.fold_in(key, 7002), 5)
    prototypes = 8
    sharpness = 1.5
    augment = 0.6
    low_end = 0.7
    high_end = 1.4
    protos = jax.random.normal(key_proto, (SUBS, prototypes, D), jnp.float32)
    mix_one = jnp.exp(sharpness * jax.random.normal(key_mix, (SUBS, NODES, prototypes), jnp.float32))
    mix_two = mix_one * jnp.exp(augment * jax.random.normal(key_augment, (SUBS, NODES, prototypes), jnp.float32))
    inverse = jax.vmap(lambda order_row: jnp.zeros((NODES,), jnp.int32).at[order_row].set(jnp.arange(NODES, dtype=jnp.int32)))(permuted)
    mix_two = jnp.take_along_axis(mix_two, inverse[:, :, None], axis=1)
    mixes = jnp.stack([mix_one, mix_two], axis=1)
    mixes = mixes / jnp.sum(mixes, axis=-1, keepdims=True)
    latent = jnp.einsum('gvnp,gpd->gvnd', mixes, protos)
    latent = latent / jnp.sqrt(jnp.mean(latent * latent, axis=-1, keepdims=True) + 1e-06)
    noise_part = jax.random.normal(key_noise, (SUBS, 2, NODES, D), jnp.float32)
    row_scale = jnp.exp(jax.random.uniform(key_scale, (SUBS, 2, NODES, 1), jnp.float32, math.log(low_end), math.log(high_end)))
    values = row_scale * (0.85 * latent + 0.53 * noise_part)
    return jnp.clip(values, -8.0, 8.0).astype(jnp.bfloat16)


def noise(rng, dims, deviation, limit, kind=jnp.bfloat16):
    return jnp.clip(deviation * jax.random.normal(rng, dims, jnp.float32), -limit, limit).astype(kind)


def setup_inputs(seed: int = 0) -> dict:
    seeds = jax.random.split(jax.random.key(seed), 6)
    return {
        "feats": draw_feats(jax.random.fold_in(seeds[5], 71), 0),
        "pos": draw_pos(jax.random.fold_in(seeds[5], 71), 0),
        "w_one": noise(seeds[2], (D, D), D ** -0.5, 0.25),
        "b_one": noise(seeds[3], (D,), 0.5, 3.0, jnp.float32),
        "w_two": noise(seeds[4], (D, D), D ** -0.5, 0.25),
    }


temper = 0.2
epsilon = 1e-06

def reference(feats, pos, w_one, b_one, w_two):
    graph_count = feats.shape[0]
    node_count = feats.shape[2]
    feat_width = feats.shape[3]
    total_rows = 2 * node_count
    block_rows = math.gcd(total_rows, 512)
    negatives = 2.0 * node_count - 2.0
    columns = jnp.arange(total_rows, dtype=jnp.int32)

    def one_graph(graph_args):
        graph_feats, graph_pos = graph_args
        rows_in = graph_feats.reshape(total_rows, feat_width)
        pre_act = jnp.dot(rows_in, w_one, preferred_element_type=jnp.float32) + b_one
        hidden = jax.nn.elu(pre_act).astype(jnp.bfloat16)
        projected = jnp.dot(hidden, w_two, preferred_element_type=jnp.float32)
        radius = jnp.sqrt(lax.optimization_barrier(jnp.sum(projected * projected, axis=1, keepdims=True)) + epsilon)
        unit_rows = projected / radius
        sent_rows = unit_rows.astype(jnp.bfloat16)
        inverse = jnp.zeros((node_count,), jnp.int32).at[graph_pos].set(jnp.arange(node_count, dtype=jnp.int32))
        partner = jnp.concatenate([graph_pos.astype(jnp.int32) + node_count, inverse])

        def score_rows(start_at):
            row_sent = lax.dynamic_slice_in_dim(sent_rows, start_at, block_rows)
            scores = jnp.dot(row_sent, sent_rows.T, preferred_element_type=jnp.float32) / temper
            partner_rows = lax.dynamic_slice_in_dim(partner, start_at, block_rows)
            row_ids = start_at + jnp.arange(block_rows, dtype=jnp.int32)
            positive = columns[None, :] == partner_rows[:, None]
            tile_coef = 2.0 * jnp.where(positive, -jax.nn.sigmoid(-scores), jax.nn.sigmoid(scores) / negatives)
            tile_coef = jnp.where(columns[None, :] == row_ids[:, None], 0.0, tile_coef).astype(jnp.bfloat16)
            return jnp.dot(tile_coef, sent_rows, preferred_element_type=jnp.float32)
        starts = jnp.arange(0, total_rows, block_rows, dtype=jnp.int32)
        grad_unit = lax.map(score_rows, starts).reshape(total_rows, feat_width) / temper
        inner_prod = lax.optimization_barrier(jnp.sum(unit_rows * grad_unit, axis=1, keepdims=True))
        grad_proj = ((grad_unit - unit_rows * inner_prod) / radius).astype(jnp.bfloat16)
        grad_hidden = jnp.dot(grad_proj, w_two.T, preferred_element_type=jnp.float32)
        elu_slope = jnp.where(pre_act > 0, 1.0, jnp.exp(jnp.minimum(pre_act, 0.0)))
        grad_pre = (grad_hidden * elu_slope).astype(jnp.bfloat16)
        grad_rows = jnp.dot(grad_pre, w_one.T, preferred_element_type=jnp.float32).astype(jnp.bfloat16)
        part_two = jnp.dot(hidden.T, grad_proj, preferred_element_type=jnp.float32)
        part_one = jnp.dot(rows_in.T, grad_pre, preferred_element_type=jnp.float32)
        part_bias = lax.optimization_barrier(jnp.sum(grad_pre.astype(jnp.float32), axis=0))
        return (grad_rows.reshape(2, node_count, feat_width), part_one, part_bias, part_two)
    grad_feats, part_one, part_bias, part_two = lax.map(one_graph, (feats, pos))
    mean_scale = 1.0 / (2.0 * node_count * graph_count)
    grad_w_one = lax.optimization_barrier(jnp.sum(part_one, axis=0)) * mean_scale
    grad_b_one = lax.optimization_barrier(jnp.sum(part_bias, axis=0)) * mean_scale
    grad_w_two = lax.optimization_barrier(jnp.sum(part_two, axis=0)) * mean_scale
    return (grad_feats, grad_w_one, grad_b_one, grad_w_two)
```

```python
import jax
import jax.numpy as jnp
from jax import lax
from jax.experimental import pallas as pl
from jax.experimental.pallas import tpu as pltpu
from jax.sharding import Mesh
from jax.sharding import PartitionSpec as P

BLK = ("yh", "x", "z")
SUB = ("yl", "co")
temper = 0.2
epsilon = 1e-06
LANES = 128


def shifted(value, axis, by):
    count = lax.axis_size(axis)
    return lax.ppermute(value, axis, [((i + by) % count, i) for i in range(count)])


def dot_nn(a, b):
    return lax.dot_general(a, b, (((1,), (0,)), ((), ())), preferred_element_type=jnp.float32)


def dot_nt(a, b):
    return lax.dot_general(a, b, (((1,), (1,)), ((), ())), preferred_element_type=jnp.float32)


def dot_tn(a, b):
    return lax.dot_general(a, b, (((0,), (0,)), ((), ())), preferred_element_type=jnp.float32)


def tile_kernel(*refs, nz, nx, ny, half, width, negatives):
    cols_count = nx * ny
    rows_ref = refs[0]
    col_refs = refs[1 : 1 + cols_count]
    w_one_ref, w_two_ref, b_one_ref, rid_ref, rpos_ref, cid_ref, cpos_ref, z_ref = refs[
        1 + cols_count : 9 + cols_count
    ]
    feats_out, weights_out, cols_s, hid_s, gp_s, pre_s = refs[9 + cols_count :]
    my_z = z_ref[0]
    for i in range(cols_count):
        for v in range(2):
            cols_s[v, i * half : (i + 1) * half, :] = col_refs[i][v * half : (v + 1) * half, :]
    w_one = w_one_ref[...]
    w_two = w_two_ref[...]
    per = 256 // half
    chunk = per * half
    for v in range(2):
        for k in range(nz // per):
            x = rows_ref[k * per : (k + 1) * per, v].reshape(chunk, width)
            row_at = slice(k * chunk, (k + 1) * chunk)
            stack_at = slice((v * nz * half) + k * chunk, (v * nz * half) + (k + 1) * chunk)
            pre = dot_nn(x, w_one) + b_one_ref[...]
            grow = jnp.exp(jnp.minimum(pre, 0.0))
            above = pre > 0
            hidden = jnp.where(above, pre, grow - 1.0).astype(jnp.bfloat16)
            slope = jnp.where(above, 1.0, grow)
            projected = dot_nn(hidden, w_two)
            radius = jnp.sqrt(jnp.sum(projected * projected, axis=1, keepdims=True) + epsilon)
            unit = projected / radius
            sent = unit.astype(jnp.bfloat16)
            rid = rid_ref[row_at, :]
            rpos = rpos_ref[row_at, :]
            total = None
            for cv in range(2):
                col = cols_s[cv]
                scores = dot_nt(sent, col) / temper
                g = jax.nn.sigmoid(scores)
                base = g * (2.0 / negatives)
                if v == cv:
                    coef = jnp.where(rid == cid_ref[...], 0.0, base)
                elif v == 0:
                    coef = jnp.where(rpos == cid_ref[...], 2.0 * g - 2.0, base)
                else:
                    coef = jnp.where(rid == cpos_ref[...], 2.0 * g - 2.0, base)
                part = dot_nn(coef.astype(jnp.bfloat16), col)
                total = part if total is None else total + part
            grad_unit = total / temper
            inner = jnp.sum(unit * grad_unit, axis=1, keepdims=True)
            grad_proj = ((grad_unit - unit * inner) / radius).astype(jnp.bfloat16)
            grad_pre = (dot_nt(grad_proj, w_two) * slope).astype(jnp.bfloat16)
            grad_rows = dot_nt(grad_pre, w_one).astype(jnp.bfloat16)
            hid_s[stack_at, :] = hidden
            gp_s[stack_at, :] = grad_proj
            pre_s[stack_at, :] = grad_pre
            for j in range(per):
                block = k * per + j
                feats_out[lax.rem(block + nz - my_z, nz), v] = grad_rows[j * half : (j + 1) * half]
    rows_all = jnp.concatenate(
        [rows_ref[:, v].reshape(nz * half, width) for v in range(2)], axis=0
    )
    part_one = dot_tn(rows_all, pre_s[...]).astype(jnp.bfloat16)
    part_two = dot_tn(hid_s[...], gp_s[...]).astype(jnp.bfloat16)
    ones = jnp.ones((2 * nz * half, LANES), jnp.bfloat16)
    part_bias = dot_tn(pre_s[...], ones).astype(jnp.bfloat16)
    per_x = width // (ny * nx)
    for yh in range(ny):
        for x in range(nx):
            source = slice((yh * nx + x) * per_x, (yh * nx + x + 1) * per_x)
            target = slice((x * ny + yh) * per_x, (x * ny + yh + 1) * per_x)
            weights_out[0, target, :width] = part_one[source]
            weights_out[0, target, width:] = part_bias[source]
            weights_out[1, target, :width] = part_two[source]
            weights_out[1, target, width:] = jnp.zeros((per_x, LANES), jnp.bfloat16)


def local(feats, pos, w_one, b_one, w_two):
    half = feats.shape[2]
    width = feats.shape[3]
    nz, nx, ny = lax.axis_size("z"), lax.axis_size("x"), lax.axis_size("yh")
    blocks = nz * nx * ny
    my_z, my_x, my_y = lax.axis_index("z"), lax.axis_index("x"), lax.axis_index("yh")
    negatives = 2.0 * half * blocks - 2.0
    own = feats[0]
    rows = lax.all_to_all(jnp.broadcast_to(own[None], (nz, *own.shape)), "z", 0, 0, tiled=True)

    flat = own.reshape(2 * half, width)
    pre_act = dot_nn(flat, w_one) + b_one
    hidden = jax.nn.elu(pre_act).astype(jnp.bfloat16)
    projected = dot_nn(hidden, w_two)
    radius = jnp.sqrt(jnp.sum(projected * projected, axis=1, keepdims=True) + epsilon)
    sent = (projected / radius).astype(jnp.bfloat16)

    cols = [sent]
    for d in range(1, ny):
        cols.append(shifted(sent, "yh", d))
    cols = [c for got in cols for c in [got] + [shifted(got, "x", d) for d in range(1, nx)]]
    col_blocks = jnp.stack(
        [((my_y + dy) % ny) * nx + (my_x + dx) % nx for dy in range(ny) for dx in range(nx)]
    )
    nodes = jnp.arange(half, dtype=jnp.int32)
    cid = ((col_blocks[:, None] * nz + my_z) * half + nodes[None, :]).reshape(1, -1)
    pos_blocks = pos[0].reshape(ny * nx, nz, half)
    cpos = lax.dynamic_index_in_dim(pos_blocks, my_z, 1, keepdims=False)[col_blocks].reshape(1, -1)
    my_yx = my_y * nx + my_x
    rid = (my_yx * (nz * half) + jnp.arange(nz * half, dtype=jnp.int32))[:, None]
    rpos = lax.dynamic_slice_in_dim(pos[0], my_yx * (nz * half), nz * half)[:, None]

    vmem = pl.BlockSpec(memory_space=pltpu.VMEM)
    count = len(cols)
    shares, weights = pl.pallas_call(
        lambda *refs: tile_kernel(
            *refs, nz=nz, nx=nx, ny=ny, half=half, width=width, negatives=negatives
        ),
        in_specs=[vmem] * (count + 8) + [pl.BlockSpec(memory_space=pltpu.SMEM)],
        out_specs=[vmem, vmem],
        out_shape=[
            jax.ShapeDtypeStruct((nz, 2, half, width), jnp.bfloat16),
            jax.ShapeDtypeStruct((2, width, width + LANES), jnp.bfloat16),
        ],
        scratch_shapes=[
            pltpu.VMEM((2, count * half, width), jnp.bfloat16),
            pltpu.VMEM((2 * nz * half, width), jnp.bfloat16),
            pltpu.VMEM((2 * nz * half, width), jnp.bfloat16),
            pltpu.VMEM((2 * nz * half, width), jnp.bfloat16),
        ],
        name="tile",
    )(rows, *cols, w_one, w_two, b_one[None], rid, rpos, cid, cpos, my_z[None])

    pieces = [shares[0]]
    for d in range(1, nz):
        pieces.append(shifted(shares[d], "z", -d))
    grad = pieces[0].astype(jnp.float32)
    for piece in pieces[1:]:
        grad = grad + piece.astype(jnp.float32)
    grad_feats = grad.astype(jnp.bfloat16)[None]

    got = lax.all_to_all(weights, "co", 0, 0, tiled=True)
    got = jnp.sum(got.astype(jnp.float32), axis=0).astype(jnp.bfloat16)
    got = lax.all_to_all(got.reshape(nx, -1, width + LANES), "x", 0, 0, tiled=True)
    got = jnp.sum(got.astype(jnp.float32), axis=0)
    got = lax.all_to_all(got.reshape(ny * nz, -1, width + LANES), ("yh", "z"), 0, 0, tiled=True)
    got = jnp.sum(got, axis=0)
    got = lax.all_to_all(
        jnp.broadcast_to(got[None], (lax.axis_size(SUB), *got.shape)), SUB, 0, 0, tiled=True
    )
    got = jnp.sum(got.reshape(lax.axis_size("yl"), 2, *got.shape[1:]), axis=0)
    got = got * (1.0 / (2.0 * half * blocks * lax.axis_size(SUB)))
    return (grad_feats, got[0, :, :width], got[0, :, width], got[1, :, :width])


def solution(mesh):
    torus = Mesh(mesh.devices.reshape(4, 2, 2, 4, 8), ("yl", "co", "yh", "x", "z"))
    in_specs = (P(SUB, None, BLK, None), P(SUB, None), P(), P(), P())
    out_specs = (P(SUB, None, BLK, None), P(BLK, None), P(BLK), P(BLK, None))
    return jax.shard_map(local, mesh=torus, in_specs=in_specs, out_specs=out_specs, check_vma=False)
```

```python
import functools

import jax
import jax.numpy as jnp
from jax import lax
from jax.experimental import pallas as pl
from jax.experimental.pallas import tpu as pltpu
from jax.sharding import Mesh
from jax.sharding import PartitionSpec as P

BLK = ("yh", "x", "z")
SUB = ("yl", "co")
temper = 0.2
epsilon = 1e-06
LANES = 128


def shifted(value, axis, by):
    count = lax.axis_size(axis)
    return lax.ppermute(value, axis, [((i + by) % count, i) for i in range(count)])


def dot_nn(a, b):
    return lax.dot_general(a, b, (((1,), (0,)), ((), ())), preferred_element_type=jnp.float32)


def dot_nt(a, b):
    return lax.dot_general(a, b, (((1,), (1,)), ((), ())), preferred_element_type=jnp.float32)


def dot_tn(a, b):
    return lax.dot_general(a, b, (((0,), (0,)), ((), ())), preferred_element_type=jnp.float32)


def tile_kernel(*refs, nz, nx, ny, half, width, negatives, order):
    groups = 6
    rows_ref = refs[0]
    col_refs = refs[1 : 1 + groups]
    w_one_ref, w_two_ref, b_one_ref, pos_ref, pos_t_ref = refs[1 + groups : 6 + groups]
    feats_out, weights_out, cols_s, hid_s, gp_s, pre_s, cpos_s = refs[6 + groups :]
    my_z, my_x, my_y = lax.axis_index("z"), lax.axis_index("x"), lax.axis_index("yh")
    my_yx = my_y * nx + my_x
    count = len(order)
    at = 0
    for ref in col_refs:
        for i in range(ref.shape[0]):
            for v in range(2):
                cols_s[v, at * half : (at + 1) * half, :] = ref[i, v * half : (v + 1) * half, :]
            at += 1
    lane = lax.broadcasted_iota(jnp.int32, (1, count * half), 1)
    cid = lax.rem(lane, half)
    for j, (dy, dx) in enumerate(order):
        block = (lax.rem(my_y + dy, ny) * nx + lax.rem(my_x + dx, nx)) * nz + my_z
        cid = cid + jnp.where(lane // half == j, block * half, 0)
        cpos_s[:, j * half : (j + 1) * half] = pos_ref[pl.ds(block, 1), :]
    cpos = cpos_s[...]
    w_one = w_one_ref[...]
    w_two = w_two_ref[...]
    per = 256 // half
    chunk = per * half
    bias = jnp.zeros((1, width), jnp.float32)
    block_lane = lax.broadcasted_iota(jnp.int32, pos_t_ref.shape, 1)
    for v in range(2):
        for k in range(nz // per):
            x = rows_ref[k * per : (k + 1) * per, v].reshape(chunk, width)
            stack_at = slice((v * nz * half) + k * chunk, (v * nz * half) + (k + 1) * chunk)
            pre = dot_nn(x, w_one) + b_one_ref[...]
            grow = jnp.exp(jnp.minimum(pre, 0.0))
            above = pre > 0
            hidden = jnp.where(above, pre, grow - 1.0).astype(jnp.bfloat16)
            slope = jnp.where(above, 1.0, grow)
            projected = dot_nn(hidden, w_two)
            radius = jnp.sqrt(jnp.sum(projected * projected, axis=1, keepdims=True) + epsilon)
            unit = projected / radius
            sent = unit.astype(jnp.bfloat16)
            first_row = (my_yx * nz + k * per) * half
            rid = first_row + lax.broadcasted_iota(jnp.int32, (chunk, 1), 0)
            if v == 0:
                rpos = jnp.concatenate(
                    [
                        jnp.sum(
                            jnp.where(block_lane == my_yx * nz + k * per + j, pos_t_ref[...], 0),
                            axis=1,
                            keepdims=True,
                        )
                        for j in range(per)
                    ],
                    axis=0,
                )
            total = None
            for cv in range(2):
                col = cols_s[cv]
                scores = dot_nt(sent, col) / temper
                g = jax.nn.sigmoid(scores)
                base = g * (2.0 / negatives)
                if v == cv:
                    coef = jnp.where(rid == cid, 0.0, base)
                elif v == 0:
                    coef = jnp.where(rpos == cid, 2.0 * g - 2.0, base)
                else:
                    coef = jnp.where(rid == cpos, 2.0 * g - 2.0, base)
                part = dot_nn(coef.astype(jnp.bfloat16), col)
                total = part if total is None else total + part
            grad_unit = total / temper
            inner = jnp.sum(unit * grad_unit, axis=1, keepdims=True)
            grad_proj = ((grad_unit - unit * inner) / radius).astype(jnp.bfloat16)
            grad_pre = (dot_nt(grad_proj, w_two) * slope).astype(jnp.bfloat16)
            grad_rows = dot_nt(grad_pre, w_one).astype(jnp.bfloat16)
            bias = bias + jnp.sum(grad_pre.astype(jnp.float32), axis=0, keepdims=True)
            hid_s[stack_at, :] = hidden
            gp_s[stack_at, :] = grad_proj
            pre_s[stack_at, :] = grad_pre
            for j in range(per):
                block = k * per + j
                feats_out[lax.rem(block + nz - my_z, nz), v] = grad_rows[j * half : (j + 1) * half]
    rows_all = jnp.concatenate(
        [rows_ref[:, v].reshape(nz * half, width) for v in range(2)], axis=0
    )
    parts = (
        dot_tn(rows_all, pre_s[...]).astype(jnp.bfloat16),
        dot_tn(hid_s[...], gp_s[...]).astype(jnp.bfloat16),
    )
    per_x = width // (ny * nx)
    rows_x = ny * per_x
    tiles = width // LANES
    tile_lane = lax.broadcasted_iota(jnp.int32, (8, LANES), 1)
    for c in range(2):
        for x in range(nx):
            piece = c * nx + x
            for t in range(tiles):
                for y in range(ny):
                    source = (y * nx + x) * per_x
                    target = t * rows_x + y * per_x
                    weights_out[piece, target : target + per_x, :] = parts[c][
                        source : source + per_x, t * LANES : (t + 1) * LANES
                    ]
            picked = []
            for y in range(ny):
                source = (y * nx + x) * per_x
                low = source // LANES * LANES
                part = jnp.broadcast_to(bias[:, low : low + LANES], (8, LANES))
                turn = (y * per_x - source) % LANES
                picked.append(pltpu.roll(part, turn, 1) if turn else part)
            row = jnp.where(tile_lane < per_x, picked[0], picked[1])
            weights_out[piece, tiles * rows_x :, :] = row.astype(jnp.bfloat16)


def first_sum(got_ref, out_ref, *, tiles, per_block, receivers):
    total = got_ref[0].astype(jnp.float32)
    for i in range(1, got_ref.shape[0]):
        total = total + got_ref[i].astype(jnp.float32)
    rows_x = receivers * per_block
    for r in range(receivers):
        picked = [
            total[t * rows_x + r * per_block : t * rows_x + (r + 1) * per_block]
            for t in range(tiles)
        ]
        picked.append(total[tiles * rows_x :])
        out_ref[r] = jnp.concatenate(picked, axis=0).astype(jnp.bfloat16)


def second_sum(got_ref, out_ref):
    total = got_ref[0].astype(jnp.float32)
    for i in range(1, got_ref.shape[0]):
        total = total + got_ref[i].astype(jnp.float32)
    for i in range(out_ref.shape[0]):
        out_ref[i] = total


def third_sum(got_ref, one_ref, two_ref, bias_ref, *, tiles, per_block, nz, scale):
    for c, ref in enumerate((one_ref, two_ref)):
        total = got_ref[c]
        for i in range(2 + c, got_ref.shape[0], 2):
            total = total + got_ref[i]
        total = total * scale
        for t in range(tiles):
            ref[:, t * LANES : (t + 1) * LANES] = total[t * per_block : (t + 1) * per_block]
        if c == 0:
            start = (lax.axis_index("yh") * nz + lax.axis_index("z")) * per_block
            last = jnp.broadcast_to(total[tiles * per_block : tiles * per_block + 1], (8, LANES))
            bias_ref[...] = pltpu.roll(last, lax.rem(LANES - start, LANES), 1)[:1]


def step(feats, pos, w_one, b_one, w_two):
    half = feats.shape[2]
    width = feats.shape[3]
    nz, nx, ny = lax.axis_size("z"), lax.axis_size("x"), lax.axis_size("yh")
    subs = lax.axis_size(SUB)
    blocks = nz * nx * ny
    negatives = 2.0 * half * blocks - 2.0
    own = feats[0]
    rows = lax.all_to_all(jnp.broadcast_to(own[None], (nz, *own.shape)), "z", 0, 0, tiled=True)

    flat = own.reshape(2 * half, width)
    pre_act = dot_nn(flat, w_one) + b_one
    hidden = jax.nn.elu(pre_act).astype(jnp.bfloat16)
    projected = dot_nn(hidden, w_two)
    radius = jnp.sqrt(jnp.sum(projected * projected, axis=1, keepdims=True) + epsilon)
    sent = (projected / radius).astype(jnp.bfloat16)[None]

    across = shifted(sent, "yh", 1)
    own_far = shifted(sent, "x", 2)
    both = jnp.concatenate([sent, across], axis=0)
    both_next = shifted(both, "x", 1)
    both_last = shifted(both, "x", 3)
    across_far = shifted(across, "x", 2)
    cols = [sent, across, both_next, both_last, own_far, across_far]
    order = [(0, 0), (1, 0), (0, 1), (1, 1), (0, 3), (1, 3), (0, 2), (1, 2)]
    pos_square = pos[0].reshape(blocks, half)

    vmem = pl.BlockSpec(memory_space=pltpu.VMEM)
    piece_rows = width // nx // 2 * 2 * (width // LANES) + 8
    shares, weights = pl.pallas_call(
        lambda *refs: tile_kernel(
            *refs, nz=nz, nx=nx, ny=ny, half=half, width=width, negatives=negatives, order=order
        ),
        in_specs=[vmem] * (len(cols) + 6),
        out_specs=[vmem, vmem],
        out_shape=[
            jax.ShapeDtypeStruct((nz, 2, half, width), jnp.bfloat16),
            jax.ShapeDtypeStruct((2 * nx, piece_rows, LANES), jnp.bfloat16),
        ],
        scratch_shapes=[
            pltpu.VMEM((2, len(order) * half, width), jnp.bfloat16),
            pltpu.VMEM((2 * nz * half, width), jnp.bfloat16),
            pltpu.VMEM((2 * nz * half, width), jnp.bfloat16),
            pltpu.VMEM((2 * nz * half, width), jnp.bfloat16),
            pltpu.VMEM((1, len(order) * half), jnp.int32),
        ],
        name="tile",
    )(rows, *cols, w_one, w_two, b_one[None], pos_square, pos_square.T)

    tiles = width // LANES
    per_block = width // blocks
    receivers = ny * nz
    short = tiles * per_block + 8
    got = lax.all_to_all(weights, ("co", "x"), 0, 0, tiled=True)
    got = pl.pallas_call(
        functools.partial(first_sum, tiles=tiles, per_block=per_block, receivers=receivers),
        in_specs=[vmem],
        out_specs=vmem,
        out_shape=jax.ShapeDtypeStruct((receivers, short, LANES), jnp.bfloat16),
        name="first_sum",
    )(got)
    got = lax.all_to_all(got, ("yh", "z"), 0, 0, tiled=True)
    got = pl.pallas_call(
        second_sum,
        in_specs=[vmem],
        out_specs=vmem,
        out_shape=jax.ShapeDtypeStruct((subs, short, LANES), jnp.float32),
        name="second_sum",
    )(got)
    got = lax.all_to_all(got, SUB, 0, 0, tiled=True)
    share_one, share_two, share_bias = pl.pallas_call(
        functools.partial(
            third_sum,
            tiles=tiles,
            per_block=per_block,
            nz=nz,
            scale=1.0 / (2.0 * half * blocks * subs),
        ),
        in_specs=[vmem],
        out_specs=[vmem] * 3,
        out_shape=[
            jax.ShapeDtypeStruct((per_block, width), jnp.float32),
            jax.ShapeDtypeStruct((per_block, width), jnp.float32),
            jax.ShapeDtypeStruct((1, LANES), jnp.float32),
        ],
        name="third_sum",
    )(got)
    share_bias = share_bias[0, :per_block]

    pieces = [shares[0]]
    for d in range(1, nz):
        pieces.append(shifted(shares[d], "z", -d))
    grad = pieces[0].astype(jnp.float32)
    for piece in pieces[1:]:
        grad = grad + piece.astype(jnp.float32)
    grad_feats = grad.astype(jnp.bfloat16)[None]
    return (grad_feats, share_one, share_bias, share_two)


def solution(mesh):
    torus = Mesh(mesh.devices.reshape(4, 2, 2, 4, 8), ("yl", "co", "yh", "x", "z"))
    in_specs = (P(SUB, None, BLK, None), P(SUB, None), P(), P(), P())
    out_specs = (P(SUB, None, BLK, None), P(BLK, None), P(BLK), P(BLK, None))
    return jax.shard_map(step, mesh=torus, in_specs=in_specs, out_specs=out_specs, check_vma=False)
```

```python
import functools

import jax
import jax.numpy as jnp
from jax import lax
from jax.experimental import pallas as pl
from jax.experimental.pallas import tpu as pltpu
from jax.sharding import Mesh
from jax.sharding import PartitionSpec as P

BLK = ("yh", "x", "z")
SUB = ("yl", "co")
temper = 0.2
epsilon = 1e-06
LANES = 128
RETURN_ORDER = (0, 3, 7, 4, 1, 6, 2, 5)


def shifted(value, axis, by):
    count = lax.axis_size(axis)
    return lax.ppermute(value, axis, [((i + by) % count, i) for i in range(count)])


def swapped(value, axis, step_by):
    count = lax.axis_size(axis)
    pairs = [(i, (i + step_by * (1 - 2 * (i % 2))) % count) for i in range(count)]
    return lax.ppermute(value, axis, pairs)


def dot_nn(a, b):
    return lax.dot_general(a, b, (((1,), (0,)), ((), ())), preferred_element_type=jnp.float32)


def dot_nt(a, b):
    return lax.dot_general(a, b, (((1,), (1,)), ((), ())), preferred_element_type=jnp.float32)


def dot_tn(a, b):
    return lax.dot_general(a, b, (((0,), (0,)), ((), ())), preferred_element_type=jnp.float32)


def tile_kernel(*refs, nz, nx, ny, half, width, negatives, order):
    groups = 6
    rows_ref = refs[0]
    col_refs = refs[1 : 1 + groups]
    w_one_ref, w_two_ref, b_one_ref, pos_ref, pos_t_ref = refs[1 + groups : 6 + groups]
    kept_out, sent_out, weights_out, x_s, cols_s, hid_s, gp_s, pre_s, cpos_s = refs[6 + groups :]
    my_z, my_x, my_y = lax.axis_index("z"), lax.axis_index("x"), lax.axis_index("yh")
    my_yx = my_y * nx + my_x
    count = len(order)
    at = 0
    for ref in col_refs:
        for i in range(ref.shape[0]):
            for v in range(2):
                cols_s[v, at * half : (at + 1) * half, :] = ref[i, v * half : (v + 1) * half, :]
            at += 1
    lane = lax.broadcasted_iota(jnp.int32, (1, count * half), 1)
    cid = lax.rem(lane, half)
    for j, (dy, dx) in enumerate(order):
        block = (lax.rem(my_y + dy, ny) * nx + lax.rem(my_x + dx, nx)) * nz + my_z
        cid = cid + jnp.where(lane // half == j, block * half, 0)
        cpos_s[:, j * half : (j + 1) * half] = pos_ref[pl.ds(block, 1), :]
    cpos = cpos_s[...]
    w_one = w_one_ref[...]
    w_two = w_two_ref[...]
    per = 256 // half
    chunk = per * half
    bias = jnp.zeros((1, width), jnp.float32)
    block_lane = lax.broadcasted_iota(jnp.int32, pos_t_ref.shape, 1)
    turn = 1 - 2 * lax.rem(my_z, 2)
    held = [lax.rem(my_z + turn * d + nz, nz) for d in RETURN_ORDER]
    half_iota = lax.broadcasted_iota(jnp.int32, (half, 1), 0)
    for v in range(2):
        for k in range(nz // per):
            blocks = held[k * per : (k + 1) * per]
            x = jnp.concatenate([rows_ref[b, v] for b in blocks], axis=0)
            stack_at = slice((v * nz * half) + k * chunk, (v * nz * half) + (k + 1) * chunk)
            pre = dot_nn(x, w_one) + b_one_ref[...]
            grow = jnp.exp(jnp.minimum(pre, 0.0))
            above = pre > 0
            hidden = jnp.where(above, pre, grow - 1.0).astype(jnp.bfloat16)
            slope = jnp.where(above, 1.0, grow)
            projected = dot_nn(hidden, w_two)
            radius = jnp.sqrt(jnp.sum(projected * projected, axis=1, keepdims=True) + epsilon)
            unit = projected / radius
            sent = unit.astype(jnp.bfloat16)
            rid = jnp.concatenate([(my_yx * nz + b) * half + half_iota for b in blocks], axis=0)
            if v == 0:
                rpos = jnp.concatenate(
                    [
                        jnp.sum(
                            jnp.where(block_lane == my_yx * nz + b, pos_t_ref[...], 0),
                            axis=1,
                            keepdims=True,
                        )
                        for b in blocks
                    ],
                    axis=0,
                )
            total = None
            for cv in range(2):
                col = cols_s[cv]
                scores = dot_nt(sent, col) / temper
                g = jax.nn.sigmoid(scores)
                base = g * (2.0 / negatives)
                if v == cv:
                    coef = jnp.where(rid == cid, 0.0, base)
                elif v == 0:
                    coef = jnp.where(rpos == cid, 2.0 * g - 2.0, base)
                else:
                    coef = jnp.where(rid == cpos, 2.0 * g - 2.0, base)
                part = dot_nn(coef.astype(jnp.bfloat16), col)
                total = part if total is None else total + part
            grad_unit = total / temper
            inner = jnp.sum(unit * grad_unit, axis=1, keepdims=True)
            grad_proj = ((grad_unit - unit * inner) / radius).astype(jnp.bfloat16)
            grad_pre = (dot_nt(grad_proj, w_two) * slope).astype(jnp.bfloat16)
            grad_rows = dot_nt(grad_pre, w_one).astype(jnp.bfloat16)
            bias = bias + jnp.sum(grad_pre.astype(jnp.float32), axis=0, keepdims=True)
            x_s[stack_at, :] = x
            hid_s[stack_at, :] = hidden
            gp_s[stack_at, :] = grad_proj
            pre_s[stack_at, :] = grad_pre
            for j in range(per):
                place = (kept_out, sent_out)[(k * per + j) * 2 // nz]
                place[(k * per + j) % (nz // 2), v] = grad_rows[j * half : (j + 1) * half]
    parts = (
        dot_tn(x_s[...], pre_s[...]).astype(jnp.bfloat16),
        dot_tn(hid_s[...], gp_s[...]).astype(jnp.bfloat16),
    )
    per_x = width // (ny * nx)
    rows_x = ny * per_x
    tiles = width // LANES
    tile_lane = lax.broadcasted_iota(jnp.int32, (8, LANES), 1)
    for c in range(2):
        for x in range(nx):
            piece = c * nx + x
            for t in range(tiles):
                for y in range(ny):
                    source = (y * nx + x) * per_x
                    target = t * rows_x + y * per_x
                    weights_out[piece, target : target + per_x, :] = parts[c][
                        source : source + per_x, t * LANES : (t + 1) * LANES
                    ]
            picked = []
            for y in range(ny):
                source = (y * nx + x) * per_x
                low = source // LANES * LANES
                part = jnp.broadcast_to(bias[:, low : low + LANES], (8, LANES))
                by = (y * per_x - source) % LANES
                picked.append(pltpu.roll(part, by, 1) if by else part)
            row = jnp.where(tile_lane < per_x, picked[0], picked[1])
            weights_out[piece, tiles * rows_x :, :] = row.astype(jnp.bfloat16)


def first_sum(got_ref, out_ref, *, tiles, per_block, receivers):
    total = got_ref[0].astype(jnp.float32)
    for i in range(1, got_ref.shape[0]):
        total = total + got_ref[i].astype(jnp.float32)
    rows_x = receivers * per_block
    for r in range(receivers):
        picked = [
            total[t * rows_x + r * per_block : t * rows_x + (r + 1) * per_block]
            for t in range(tiles)
        ]
        picked.append(total[tiles * rows_x :])
        out_ref[r] = jnp.concatenate(picked, axis=0).astype(jnp.bfloat16)


def second_sum(got_ref, out_ref):
    total = got_ref[0].astype(jnp.float32)
    for i in range(1, got_ref.shape[0]):
        total = total + got_ref[i].astype(jnp.float32)
    for i in range(out_ref.shape[0]):
        out_ref[i] = total


def third_sum(got_ref, one_ref, two_ref, bias_ref, *, tiles, per_block, nz, scale):
    for c, ref in enumerate((one_ref, two_ref)):
        total = got_ref[c]
        for i in range(2 + c, got_ref.shape[0], 2):
            total = total + got_ref[i]
        total = total * scale
        for t in range(tiles):
            ref[:, t * LANES : (t + 1) * LANES] = total[t * per_block : (t + 1) * per_block]
        if c == 0:
            start = (lax.axis_index("yh") * nz + lax.axis_index("z")) * per_block
            last = jnp.broadcast_to(total[tiles * per_block : tiles * per_block + 1], (8, LANES))
            bias_ref[...] = pltpu.roll(last, lax.rem(LANES - start, LANES), 1)[:1]


def step(feats, pos, w_one, b_one, w_two):
    half = feats.shape[2]
    width = feats.shape[3]
    nz, nx, ny = lax.axis_size("z"), lax.axis_size("x"), lax.axis_size("yh")
    subs = lax.axis_size(SUB)
    blocks = nz * nx * ny
    negatives = 2.0 * half * blocks - 2.0
    own = feats[0]
    rows = lax.all_to_all(jnp.broadcast_to(own[None], (nz, *own.shape)), "z", 0, 0, tiled=True)

    flat = own.reshape(2 * half, width)
    pre_act = dot_nn(flat, w_one) + b_one
    hidden = jax.nn.elu(pre_act).astype(jnp.bfloat16)
    projected = dot_nn(hidden, w_two)
    radius = jnp.sqrt(jnp.sum(projected * projected, axis=1, keepdims=True) + epsilon)
    sent = (projected / radius).astype(jnp.bfloat16)[None]

    across = shifted(sent, "yh", 1)
    own_far = shifted(sent, "x", 2)
    both = jnp.concatenate([sent, across], axis=0)
    both_next = shifted(both, "x", 1)
    both_last = shifted(both, "x", 3)
    across_far = shifted(across, "x", 2)
    cols = [sent, across, both_next, both_last, own_far, across_far]
    order = [(0, 0), (1, 0), (0, 1), (1, 1), (0, 3), (1, 3), (0, 2), (1, 2)]
    pos_square = pos[0].reshape(blocks, half)

    vmem = pl.BlockSpec(memory_space=pltpu.VMEM)
    piece_rows = width // nx // 2 * 2 * (width // LANES) + 8
    kept, sent_back, weights = pl.pallas_call(
        lambda *refs: tile_kernel(
            *refs, nz=nz, nx=nx, ny=ny, half=half, width=width, negatives=negatives, order=order
        ),
        in_specs=[vmem] * (len(cols) + 6),
        out_specs=[vmem, vmem, vmem],
        out_shape=[
            jax.ShapeDtypeStruct((nz // 2, 2, half, width), jnp.bfloat16),
            jax.ShapeDtypeStruct((nz // 2, 2, half, width), jnp.bfloat16),
            jax.ShapeDtypeStruct((2 * nx, piece_rows, LANES), jnp.bfloat16),
        ],
        scratch_shapes=[
            pltpu.VMEM((2 * nz * half, width), jnp.bfloat16),
            pltpu.VMEM((2, len(order) * half, width), jnp.bfloat16),
            pltpu.VMEM((2 * nz * half, width), jnp.bfloat16),
            pltpu.VMEM((2 * nz * half, width), jnp.bfloat16),
            pltpu.VMEM((2 * nz * half, width), jnp.bfloat16),
            pltpu.VMEM((1, len(order) * half), jnp.int32),
        ],
        name="tile",
    )(rows, *cols, w_one, w_two, b_one[None], pos_square, pos_square.T)

    tiles = width // LANES
    per_block = width // blocks
    receivers = ny * nz
    short = tiles * per_block + 8
    got = lax.all_to_all(weights, ("co", "x"), 0, 0, tiled=True)
    got = pl.pallas_call(
        functools.partial(first_sum, tiles=tiles, per_block=per_block, receivers=receivers),
        in_specs=[vmem],
        out_specs=vmem,
        out_shape=jax.ShapeDtypeStruct((receivers, short, LANES), jnp.bfloat16),
        name="first_sum",
    )(got)
    got = lax.all_to_all(got, ("yh", "z"), 0, 0, tiled=True)
    got = pl.pallas_call(
        second_sum,
        in_specs=[vmem],
        out_specs=vmem,
        out_shape=jax.ShapeDtypeStruct((subs, short, LANES), jnp.float32),
        name="second_sum",
    )(got)
    got = lax.all_to_all(got, SUB, 0, 0, tiled=True)
    share_one, share_two, share_bias = pl.pallas_call(
        functools.partial(
            third_sum,
            tiles=tiles,
            per_block=per_block,
            nz=nz,
            scale=1.0 / (2.0 * half * blocks * subs),
        ),
        in_specs=[vmem],
        out_specs=[vmem] * 3,
        out_shape=[
            jax.ShapeDtypeStruct((per_block, width), jnp.float32),
            jax.ShapeDtypeStruct((per_block, width), jnp.float32),
            jax.ShapeDtypeStruct((1, LANES), jnp.float32),
        ],
        name="third_sum",
    )(got)
    share_bias = share_bias[0, :per_block]

    grad = kept
    moved = sent_back
    for i, step_by in enumerate((1, -1, 3)):
        moved = swapped(moved, "z", step_by)
        grad = grad.astype(jnp.float32) + moved.astype(jnp.float32)
        if i < 2:
            moved = grad[grad.shape[0] // 2 :].astype(jnp.bfloat16)
            grad = grad[: grad.shape[0] // 2]
    grad_feats = grad.astype(jnp.bfloat16)
    return (grad_feats, share_one, share_bias, share_two)


def solution(mesh):
    torus = Mesh(mesh.devices.reshape(4, 2, 2, 4, 8), ("yl", "co", "yh", "x", "z"))
    in_specs = (P(SUB, None, BLK, None), P(SUB, None), P(), P(), P())
    out_specs = (P(SUB, None, BLK, None), P(BLK, None), P(BLK), P(BLK, None))
    return jax.shard_map(step, mesh=torus, in_specs=in_specs, out_specs=out_specs, check_vma=False)
```

```python
import functools

import jax
import jax.numpy as jnp
from jax import lax
from jax.experimental import pallas as pl
from jax.experimental.pallas import tpu as pltpu
from jax.sharding import Mesh
from jax.sharding import PartitionSpec as P

BLK = ("yh", "x", "z")
SUB = ("yl", "co")
temper = 0.2
epsilon = 1e-06
LANES = 128
VMEM_LIMIT = 24 * 2**20
RETURN_ORDER = (0, 3, 7, 4, 1, 6, 2, 5)


def shifted(value, axis, by):
    count = lax.axis_size(axis)
    return lax.ppermute(value, axis, [((i + by) % count, i) for i in range(count)])


def in_vmem(value):
    return pltpu.with_memory_space_constraint(value, pltpu.VMEM)


def swapped(value, axis, step_by):
    count = lax.axis_size(axis)
    pairs = [(i, (i + step_by * (1 - 2 * (i % 2))) % count) for i in range(count)]
    return lax.ppermute(value, axis, pairs)


def dot_nn(a, b):
    return lax.dot_general(a, b, (((1,), (0,)), ((), ())), preferred_element_type=jnp.float32)


def dot_nt(a, b):
    return lax.dot_general(a, b, (((1,), (1,)), ((), ())), preferred_element_type=jnp.float32)


def dot_tn(a, b):
    return lax.dot_general(a, b, (((0,), (0,)), ((), ())), preferred_element_type=jnp.float32)


def tile_kernel(*refs, nz, nx, ny, half, width, negatives, order):
    groups = 6
    rows_ref = refs[0]
    col_refs = refs[1 : 1 + groups]
    w_one_ref, w_two_ref, b_one_ref, pos_ref, pos_t_ref = refs[1 + groups : 6 + groups]
    kept_out, sent_out, weights_out, x_s, cols_s, hid_s, gp_s, pre_s, cpos_s = refs[6 + groups :]
    my_z, my_x, my_y = lax.axis_index("z"), lax.axis_index("x"), lax.axis_index("yh")
    my_yx = my_y * nx + my_x
    count = len(order)
    at = 0
    for ref in col_refs:
        for i in range(ref.shape[0]):
            for v in range(2):
                cols_s[v, at * half : (at + 1) * half, :] = ref[i, v * half : (v + 1) * half, :]
            at += 1
    lane = lax.broadcasted_iota(jnp.int32, (1, count * half), 1)
    cid = lax.rem(lane, half)
    for j, (dy, dx) in enumerate(order):
        block = (lax.rem(my_y + dy, ny) * nx + lax.rem(my_x + dx, nx)) * nz + my_z
        cid = cid + jnp.where(lane // half == j, block * half, 0)
        cpos_s[:, j * half : (j + 1) * half] = pos_ref[pl.ds(block, 1), :]
    cpos = cpos_s[...]
    w_one = w_one_ref[...]
    w_two = w_two_ref[...]
    per = 256 // half
    chunk = per * half
    bias = jnp.zeros((1, width), jnp.float32)
    block_lane = lax.broadcasted_iota(jnp.int32, pos_t_ref.shape, 1)
    turn = 1 - 2 * lax.rem(my_z, 2)
    held = [lax.rem(my_z + turn * d + nz, nz) for d in RETURN_ORDER]
    half_iota = lax.broadcasted_iota(jnp.int32, (half, 1), 0)
    for v in range(2):
        for k in range(nz // per):
            blocks = held[k * per : (k + 1) * per]
            x = jnp.concatenate([rows_ref[b, v] for b in blocks], axis=0)
            stack_at = slice((v * nz * half) + k * chunk, (v * nz * half) + (k + 1) * chunk)
            pre = dot_nn(x, w_one) + b_one_ref[...]
            grow = jnp.exp(jnp.minimum(pre, 0.0))
            above = pre > 0
            hidden = jnp.where(above, pre, grow - 1.0).astype(jnp.bfloat16)
            slope = jnp.where(above, 1.0, grow)
            projected = dot_nn(hidden, w_two)
            radius = jnp.sqrt(jnp.sum(projected * projected, axis=1, keepdims=True) + epsilon)
            unit = projected / radius
            sent = unit.astype(jnp.bfloat16)
            rid = jnp.concatenate([(my_yx * nz + b) * half + half_iota for b in blocks], axis=0)
            if v == 0:
                rpos = jnp.concatenate(
                    [
                        jnp.sum(
                            jnp.where(block_lane == my_yx * nz + b, pos_t_ref[...], 0),
                            axis=1,
                            keepdims=True,
                        )
                        for b in blocks
                    ],
                    axis=0,
                )
            total = None
            for cv in range(2):
                col = cols_s[cv]
                scores = dot_nt(sent, col) / temper
                g = jax.nn.sigmoid(scores)
                base = g * (2.0 / negatives)
                if v == cv:
                    coef = jnp.where(rid == cid, 0.0, base)
                elif v == 0:
                    coef = jnp.where(rpos == cid, 2.0 * g - 2.0, base)
                else:
                    coef = jnp.where(rid == cpos, 2.0 * g - 2.0, base)
                part = dot_nn(coef.astype(jnp.bfloat16), col)
                total = part if total is None else total + part
            grad_unit = total / temper
            inner = jnp.sum(unit * grad_unit, axis=1, keepdims=True)
            grad_proj = ((grad_unit - unit * inner) / radius).astype(jnp.bfloat16)
            grad_pre = (dot_nt(grad_proj, w_two) * slope).astype(jnp.bfloat16)
            grad_rows = dot_nt(grad_pre, w_one).astype(jnp.bfloat16)
            bias = bias + jnp.sum(grad_pre.astype(jnp.float32), axis=0, keepdims=True)
            x_s[stack_at, :] = x
            hid_s[stack_at, :] = hidden
            gp_s[stack_at, :] = grad_proj
            pre_s[stack_at, :] = grad_pre
            for j in range(per):
                place = (kept_out, sent_out)[(k * per + j) * 2 // nz]
                place[(k * per + j) % (nz // 2), v] = grad_rows[j * half : (j + 1) * half]
    parts = (
        dot_tn(x_s[...], pre_s[...]).astype(jnp.bfloat16),
        dot_tn(hid_s[...], gp_s[...]).astype(jnp.bfloat16),
    )
    per_x = width // (ny * nx)
    rows_x = ny * per_x
    tiles = width // LANES
    tile_lane = lax.broadcasted_iota(jnp.int32, (8, LANES), 1)
    for c in range(2):
        for x in range(nx):
            piece = c * nx + x
            for t in range(tiles):
                for y in range(ny):
                    source = (y * nx + x) * per_x
                    target = t * rows_x + y * per_x
                    weights_out[piece, target : target + per_x, :] = parts[c][
                        source : source + per_x, t * LANES : (t + 1) * LANES
                    ]
            picked = []
            for y in range(ny):
                source = (y * nx + x) * per_x
                low = source // LANES * LANES
                part = jnp.broadcast_to(bias[:, low : low + LANES], (8, LANES))
                by = (y * per_x - source) % LANES
                picked.append(pltpu.roll(part, by, 1) if by else part)
            row = jnp.where(tile_lane < per_x, picked[0], picked[1])
            weights_out[piece, tiles * rows_x :, :] = row.astype(jnp.bfloat16)


def spread(own_ref, out_ref):
    for i in range(out_ref.shape[0]):
        out_ref[i] = own_ref[...]


def first_sum(got_ref, out_ref, *, tiles, per_block, receivers):
    total = got_ref[0].astype(jnp.float32)
    for i in range(1, got_ref.shape[0]):
        total = total + got_ref[i].astype(jnp.float32)
    rows_x = receivers * per_block
    for r in range(receivers):
        picked = [
            total[t * rows_x + r * per_block : t * rows_x + (r + 1) * per_block]
            for t in range(tiles)
        ]
        picked.append(total[tiles * rows_x :])
        out_ref[r] = jnp.concatenate(picked, axis=0).astype(jnp.bfloat16)


def second_sum(got_ref, out_ref):
    total = got_ref[0].astype(jnp.float32)
    for i in range(1, got_ref.shape[0]):
        total = total + got_ref[i].astype(jnp.float32)
    total = total.astype(jnp.bfloat16)
    for i in range(out_ref.shape[0]):
        out_ref[i] = total


def third_sum(got_ref, one_ref, two_ref, bias_ref, *, tiles, per_block, nz, scale):
    for c, ref in enumerate((one_ref, two_ref)):
        total = got_ref[c].astype(jnp.float32)
        for i in range(2 + c, got_ref.shape[0], 2):
            total = total + got_ref[i].astype(jnp.float32)
        total = total * scale
        for t in range(tiles):
            ref[:, t * LANES : (t + 1) * LANES] = total[t * per_block : (t + 1) * per_block]
        if c == 0:
            start = (lax.axis_index("yh") * nz + lax.axis_index("z")) * per_block
            last = jnp.broadcast_to(total[tiles * per_block : tiles * per_block + 1], (8, LANES))
            last = pltpu.roll(last, lax.rem(LANES - start, LANES), 1)
            bias_ref[...] = last[0, :per_block]


def step(feats, pos, w_one, b_one, w_two):
    half = feats.shape[2]
    width = feats.shape[3]
    nz, nx, ny = lax.axis_size("z"), lax.axis_size("x"), lax.axis_size("yh")
    subs = lax.axis_size(SUB)
    blocks = nz * nx * ny
    negatives = 2.0 * half * blocks - 2.0
    own = feats[0]
    vmem = pl.BlockSpec(memory_space=pltpu.VMEM)
    copies = pl.pallas_call(
        spread,
        in_specs=[vmem],
        out_specs=vmem,
        out_shape=jax.ShapeDtypeStruct((nz, *own.shape), own.dtype),
        name="spread",
    )(own)
    rows = lax.all_to_all(copies, "z", 0, 0, tiled=True)

    flat = own.reshape(2 * half, width)
    pre_act = dot_nn(flat, w_one) + b_one
    hidden = jax.nn.elu(pre_act).astype(jnp.bfloat16)
    projected = dot_nn(hidden, w_two)
    radius = jnp.sqrt(jnp.sum(projected * projected, axis=1, keepdims=True) + epsilon)
    sent = (projected / radius).astype(jnp.bfloat16)[None]

    across = shifted(sent, "yh", 1)
    own_far = shifted(sent, "x", 2)
    both = jnp.concatenate([sent, across], axis=0)
    both_next = shifted(both, "x", 1)
    both_last = shifted(both, "x", 3)
    across_far = shifted(across, "x", 2)
    cols = [sent, across, both_next, both_last, own_far, across_far]
    order = [(0, 0), (1, 0), (0, 1), (1, 1), (0, 3), (1, 3), (0, 2), (1, 2)]
    pos_square = pos[0].reshape(blocks, half)

    piece_rows = width // nx // 2 * 2 * (width // LANES) + 8
    kept, sent_back, weights = pl.pallas_call(
        lambda *refs: tile_kernel(
            *refs, nz=nz, nx=nx, ny=ny, half=half, width=width, negatives=negatives, order=order
        ),
        in_specs=[vmem] * (len(cols) + 6),
        out_specs=[vmem, vmem, vmem],
        out_shape=[
            jax.ShapeDtypeStruct((nz // 2, 2, half, width), jnp.bfloat16),
            jax.ShapeDtypeStruct((nz // 2, 2, half, width), jnp.bfloat16),
            jax.ShapeDtypeStruct((2 * nx, piece_rows, LANES), jnp.bfloat16),
        ],
        scratch_shapes=[
            pltpu.VMEM((2 * nz * half, width), jnp.bfloat16),
            pltpu.VMEM((2, len(order) * half, width), jnp.bfloat16),
            pltpu.VMEM((2 * nz * half, width), jnp.bfloat16),
            pltpu.VMEM((2 * nz * half, width), jnp.bfloat16),
            pltpu.VMEM((2 * nz * half, width), jnp.bfloat16),
            pltpu.VMEM((1, len(order) * half), jnp.int32),
        ],
        compiler_params=pltpu.CompilerParams(vmem_limit_bytes=VMEM_LIMIT),
        name="tile",
    )(*map(in_vmem, (rows, *cols, w_one, w_two, b_one[None], pos_square, pos_square.T)))

    tiles = width // LANES
    per_block = width // blocks
    receivers = ny * nz
    short = tiles * per_block + 8
    got = lax.all_to_all(weights, ("co", "x"), 0, 0, tiled=True)
    got = pl.pallas_call(
        functools.partial(first_sum, tiles=tiles, per_block=per_block, receivers=receivers),
        in_specs=[vmem],
        out_specs=vmem,
        out_shape=jax.ShapeDtypeStruct((receivers, short, LANES), jnp.bfloat16),
        name="first_sum",
    )(in_vmem(got))
    got = lax.all_to_all(got, ("yh", "z"), 0, 0, tiled=True)
    got = pl.pallas_call(
        second_sum,
        in_specs=[vmem],
        out_specs=vmem,
        out_shape=jax.ShapeDtypeStruct((subs, short, LANES), jnp.bfloat16),
        name="second_sum",
    )(in_vmem(got))
    got = lax.all_to_all(got, SUB, 0, 0, tiled=True)
    share_one, share_two, share_bias = pl.pallas_call(
        functools.partial(
            third_sum,
            tiles=tiles,
            per_block=per_block,
            nz=nz,
            scale=1.0 / (2.0 * half * blocks * subs),
        ),
        in_specs=[vmem],
        out_specs=[vmem] * 3,
        out_shape=[
            jax.ShapeDtypeStruct((per_block, width), jnp.float32),
            jax.ShapeDtypeStruct((per_block, width), jnp.float32),
            jax.ShapeDtypeStruct((per_block,), jnp.float32),
        ],
        name="third_sum",
    )(in_vmem(got))

    grad = kept
    moved = sent_back
    for i, step_by in enumerate((1, -1, 3)):
        moved = swapped(moved, "z", step_by)
        grad = grad.astype(jnp.float32) + moved.astype(jnp.float32)
        if i < 2:
            moved = grad[grad.shape[0] // 2 :].astype(jnp.bfloat16)
            grad = grad[: grad.shape[0] // 2]
    grad_feats = grad.astype(jnp.bfloat16)
    return (grad_feats, share_one, share_bias, share_two)


def solution(mesh):
    torus = Mesh(mesh.devices.reshape(4, 2, 2, 4, 8), ("yl", "co", "yh", "x", "z"))
    in_specs = (P(SUB, None, BLK, None), P(SUB, None), P(), P(), P())
    out_specs = (P(SUB, None, BLK, None), P(BLK, None), P(BLK), P(BLK, None))
    return jax.shard_map(step, mesh=torus, in_specs=in_specs, out_specs=out_specs, check_vma=False)
```

```python
import functools

import jax
import jax.numpy as jnp
from jax import lax
from jax.experimental import pallas as pl
from jax.experimental.pallas import tpu as pltpu
from jax.sharding import Mesh
from jax.sharding import PartitionSpec as P

BLK = ("yh", "x", "z")
SUB = ("yl", "co")
temper = 0.2
epsilon = 1e-06
LANES = 128
VMEM_LIMIT = 24 * 2**20
RETURN_ORDER = (0, 3, 7, 4, 1, 6, 2, 5)


def shifted(value, axis, by):
    count = lax.axis_size(axis)
    return lax.ppermute(value, axis, [((i + by) % count, i) for i in range(count)])


def in_vmem(value):
    return pltpu.with_memory_space_constraint(value, pltpu.VMEM)


def in_hbm(value):
    return pltpu.with_memory_space_constraint(value, pltpu.HBM)


def swapped(value, axis, step_by):
    count = lax.axis_size(axis)
    pairs = [(i, (i + step_by * (1 - 2 * (i % 2))) % count) for i in range(count)]
    return lax.ppermute(value, axis, pairs)


def dot_nn(a, b):
    return lax.dot_general(a, b, (((1,), (0,)), ((), ())), preferred_element_type=jnp.float32)


def dot_nt(a, b):
    return lax.dot_general(a, b, (((1,), (1,)), ((), ())), preferred_element_type=jnp.float32)


def dot_tn(a, b):
    return lax.dot_general(a, b, (((0,), (0,)), ((), ())), preferred_element_type=jnp.float32)


def pos_of(pos_ref, block):
    start = pl.multiple_of(block // 2 * LANES, LANES)
    pair = jnp.broadcast_to(pos_ref[:, pl.ds(start, LANES)], (8, LANES))
    return jnp.where(lax.rem(block, 2) == 1, pltpu.roll(pair, LANES // 2, 1), pair)


def rows_kernel(pre_ref, w_one_ref, kept_out, sent_out, *, nz, half):
    w_one = w_one_ref[...]
    per = nz // 2
    chunk = per * half
    for k, out in ((1, sent_out), (0, kept_out)):
        for v in range(2):
            start = (v * 2 + k) * chunk
            rows = dot_nt(pre_ref[start : start + chunk, :], w_one).astype(jnp.bfloat16)
            for j in range(per):
                out[j, v] = rows[j * half : (j + 1) * half]


def tile_kernel(*refs, nz, nx, ny, half, width, negatives, order):
    groups = 6
    rows_ref = refs[0]
    col_refs = refs[1 : 1 + groups]
    w_one_ref, w_two_ref, b_one_ref, pos_ref = refs[1 + groups : 5 + groups]
    pre_s, weights_out, cols_s, x_s, hid_s, gp_s, cpos_s = refs[5 + groups :]
    my_z, my_x, my_y = lax.axis_index("z"), lax.axis_index("x"), lax.axis_index("yh")
    my_yx = my_y * nx + my_x
    count = len(order)
    at = 0
    for ref in col_refs:
        for i in range(ref.shape[0]):
            for v in range(2):
                cols_s[v, at * half : (at + 1) * half, :] = ref[i, v * half : (v + 1) * half, :]
            at += 1
    lane = lax.broadcasted_iota(jnp.int32, (1, count * half), 1)
    cid = lax.rem(lane, half)
    for j, (dy, dx) in enumerate(order):
        block = (lax.rem(my_y + dy, ny) * nx + lax.rem(my_x + dx, nx)) * nz + my_z
        cid = cid + jnp.where(lane // half == j, block * half, 0)
        cpos_s[:, j * half : (j + 1) * half] = pos_of(pos_ref, block)[:1, :half]
    cpos = cpos_s[...]
    w_one = w_one_ref[...]
    w_two = w_two_ref[...]
    per = 256 // half
    chunk = per * half
    bias = jnp.zeros((1, width), jnp.float32)
    diagonal = lax.broadcasted_iota(jnp.int32, (half, LANES), 0) == lax.broadcasted_iota(
        jnp.int32, (half, LANES), 1
    )
    turn = 1 - 2 * lax.rem(my_z, 2)
    held = [lax.rem(my_z + turn * d + nz, nz) for d in RETURN_ORDER]
    half_iota = lax.broadcasted_iota(jnp.int32, (half, 1), 0)
    for v in range(2):
        for k in range(nz // per):
            blocks = held[k * per : (k + 1) * per]
            x = jnp.concatenate([rows_ref[b, v] for b in blocks], axis=0)
            stack_at = slice((v * nz * half) + k * chunk, (v * nz * half) + (k + 1) * chunk)
            pre = dot_nn(x, w_one) + b_one_ref[...]
            grow = jnp.exp(jnp.minimum(pre, 0.0))
            above = pre > 0
            hidden = jnp.where(above, pre, grow - 1.0).astype(jnp.bfloat16)
            slope = jnp.where(above, 1.0, grow)
            projected = dot_nn(hidden, w_two)
            radius = jnp.sqrt(jnp.sum(projected * projected, axis=1, keepdims=True) + epsilon)
            unit = projected / radius
            sent = unit.astype(jnp.bfloat16)
            rid = jnp.concatenate([(my_yx * nz + b) * half + half_iota for b in blocks], axis=0)
            if v == 0:
                rpos = jnp.concatenate(
                    [
                        jnp.sum(
                            jnp.where(diagonal, pos_of(pos_ref, my_yx * nz + b)[:1], 0),
                            axis=1,
                            keepdims=True,
                        )
                        for b in blocks
                    ],
                    axis=0,
                )
            total = None
            for cv in range(2):
                col = cols_s[cv]
                scores = dot_nt(sent, col) / temper
                g = jax.nn.sigmoid(scores)
                base = g * (2.0 / negatives)
                if v == cv:
                    coef = jnp.where(rid == cid, 0.0, base)
                elif v == 0:
                    coef = jnp.where(rpos == cid, 2.0 * g - 2.0, base)
                else:
                    coef = jnp.where(rid == cpos, 2.0 * g - 2.0, base)
                part = dot_nn(coef.astype(jnp.bfloat16), col)
                total = part if total is None else total + part
            grad_unit = total / temper
            inner = jnp.sum(unit * grad_unit, axis=1, keepdims=True)
            grad_proj = ((grad_unit - unit * inner) / radius).astype(jnp.bfloat16)
            grad_pre = (dot_nt(grad_proj, w_two) * slope).astype(jnp.bfloat16)
            bias = bias + jnp.sum(grad_pre.astype(jnp.float32), axis=0, keepdims=True)
            x_s[stack_at, :] = x
            hid_s[stack_at, :] = hidden
            gp_s[stack_at, :] = grad_proj
            pre_s[stack_at, :] = grad_pre
    parts = (
        dot_tn(x_s[...], pre_s[...]).astype(jnp.bfloat16),
        dot_tn(hid_s[...], gp_s[...]).astype(jnp.bfloat16),
    )
    per_x = width // (ny * nx)
    rows_x = ny * per_x
    tiles = width // LANES
    tile_lane = lax.broadcasted_iota(jnp.int32, (8, LANES), 1)
    for c in range(2):
        for x in range(nx):
            piece = c * nx + x
            for t in range(tiles):
                for y in range(ny):
                    source = (y * nx + x) * per_x
                    target = t * rows_x + y * per_x
                    weights_out[piece, target : target + per_x, :] = parts[c][
                        source : source + per_x, t * LANES : (t + 1) * LANES
                    ]
            picked = []
            for y in range(ny):
                source = (y * nx + x) * per_x
                low = source // LANES * LANES
                part = jnp.broadcast_to(bias[:, low : low + LANES], (8, LANES))
                by = (y * per_x - source) % LANES
                picked.append(pltpu.roll(part, by, 1) if by else part)
            row = jnp.where(tile_lane < per_x, picked[0], picked[1])
            weights_out[piece, tiles * rows_x :, :] = row.astype(jnp.bfloat16)


def spread(own_ref, out_ref):
    for i in range(out_ref.shape[0]):
        out_ref[i] = own_ref[...]


def first_sum(got_ref, out_ref, *, tiles, per_block, receivers):
    total = got_ref[0].astype(jnp.float32)
    for i in range(1, got_ref.shape[0]):
        total = total + got_ref[i].astype(jnp.float32)
    rows_x = receivers * per_block
    for r in range(receivers):
        picked = [
            total[t * rows_x + r * per_block : t * rows_x + (r + 1) * per_block]
            for t in range(tiles)
        ]
        picked.append(total[tiles * rows_x :])
        out_ref[r] = jnp.concatenate(picked, axis=0).astype(jnp.bfloat16)


def second_sum(got_ref, out_ref):
    total = got_ref[0].astype(jnp.float32)
    for i in range(1, got_ref.shape[0]):
        total = total + got_ref[i].astype(jnp.float32)
    total = total.astype(jnp.bfloat16)
    for i in range(out_ref.shape[0]):
        out_ref[i] = total


def third_sum(got_ref, one_ref, two_ref, bias_ref, *, tiles, per_block, nz, scale):
    for c, ref in enumerate((one_ref, two_ref)):
        total = got_ref[c].astype(jnp.float32)
        for i in range(2 + c, got_ref.shape[0], 2):
            total = total + got_ref[i].astype(jnp.float32)
        total = total * scale
        for t in range(tiles):
            ref[:, t * LANES : (t + 1) * LANES] = total[t * per_block : (t + 1) * per_block]
        if c == 0:
            start = (lax.axis_index("yh") * nz + lax.axis_index("z")) * per_block
            last = jnp.broadcast_to(total[tiles * per_block : tiles * per_block + 1], (8, LANES))
            last = pltpu.roll(last, lax.rem(LANES - start, LANES), 1)
            bias_ref[...] = last[0, :per_block]


def step(feats, pos, w_one, b_one, w_two):
    half = feats.shape[2]
    width = feats.shape[3]
    nz, nx, ny = lax.axis_size("z"), lax.axis_size("x"), lax.axis_size("yh")
    subs = lax.axis_size(SUB)
    blocks = nz * nx * ny
    negatives = 2.0 * half * blocks - 2.0
    own = feats[0]
    vmem = pl.BlockSpec(memory_space=pltpu.VMEM)
    copies = pl.pallas_call(
        spread,
        in_specs=[vmem],
        out_specs=vmem,
        out_shape=jax.ShapeDtypeStruct((nz, *own.shape), own.dtype),
        name="spread",
    )(own)
    rows = lax.all_to_all(copies, "z", 0, 0, tiled=True)

    flat = own.reshape(2 * half, width)
    pre_act = dot_nn(flat, w_one) + b_one
    hidden = jax.nn.elu(pre_act).astype(jnp.bfloat16)
    projected = dot_nn(hidden, w_two)
    radius = jnp.sqrt(jnp.sum(projected * projected, axis=1, keepdims=True) + epsilon)
    sent = (projected / radius).astype(jnp.bfloat16)[None]

    across = shifted(sent, "yh", 1)
    own_far = shifted(sent, "x", 2)
    both = jnp.concatenate([sent, across], axis=0)
    both_next = shifted(both, "x", 1)
    both_last = shifted(both, "x", 3)
    across_far = shifted(across, "x", 2)
    cols = [sent, across, both_next, both_last, own_far, across_far]
    order = [(0, 0), (1, 0), (0, 1), (1, 1), (0, 3), (1, 3), (0, 2), (1, 2)]
    piece_rows = width // nx // 2 * 2 * (width // LANES) + 8
    pre, weights = pl.pallas_call(
        lambda *refs: tile_kernel(
            *refs, nz=nz, nx=nx, ny=ny, half=half, width=width, negatives=negatives, order=order
        ),
        in_specs=[vmem] * (len(cols) + 5),
        out_specs=[vmem, vmem],
        out_shape=[
            jax.ShapeDtypeStruct((2 * nz * half, width), jnp.bfloat16),
            jax.ShapeDtypeStruct((2 * nx, piece_rows, LANES), jnp.bfloat16),
        ],
        scratch_shapes=[
            pltpu.VMEM((2, len(order) * half, width), jnp.bfloat16),
            pltpu.VMEM((2 * nz * half, width), jnp.bfloat16),
            pltpu.VMEM((2 * nz * half, width), jnp.bfloat16),
            pltpu.VMEM((2 * nz * half, width), jnp.bfloat16),
            pltpu.VMEM((1, len(order) * half), jnp.int32),
        ],
        compiler_params=pltpu.CompilerParams(vmem_limit_bytes=VMEM_LIMIT),
        name="tile",
    )(in_vmem(rows), in_vmem(cols[0]), in_vmem(cols[1]), in_hbm(cols[2]), in_hbm(cols[3]), in_vmem(cols[4]), in_hbm(cols[5]), *map(in_vmem, (w_one, w_two, b_one[None], pos)))

    tiles = width // LANES
    per_block = width // blocks
    receivers = ny * nz
    short = tiles * per_block + 8
    got = lax.all_to_all(weights, ("co", "x"), 0, 0, tiled=True)
    got = pl.pallas_call(
        functools.partial(first_sum, tiles=tiles, per_block=per_block, receivers=receivers),
        in_specs=[vmem],
        out_specs=vmem,
        out_shape=jax.ShapeDtypeStruct((receivers, short, LANES), jnp.bfloat16),
        name="first_sum",
    )(in_vmem(got))
    got = lax.all_to_all(got, ("yh", "z"), 0, 0, tiled=True)
    got = pl.pallas_call(
        second_sum,
        in_specs=[vmem],
        out_specs=vmem,
        out_shape=jax.ShapeDtypeStruct((subs, short, LANES), jnp.bfloat16),
        name="second_sum",
    )(in_vmem(got))
    got = lax.all_to_all(got, SUB, 0, 0, tiled=True)
    share_one, share_two, share_bias = pl.pallas_call(
        functools.partial(
            third_sum,
            tiles=tiles,
            per_block=per_block,
            nz=nz,
            scale=1.0 / (2.0 * half * blocks * subs),
        ),
        in_specs=[vmem],
        out_specs=[vmem] * 3,
        out_shape=[
            jax.ShapeDtypeStruct((per_block, width), jnp.float32),
            jax.ShapeDtypeStruct((per_block, width), jnp.float32),
            jax.ShapeDtypeStruct((per_block,), jnp.float32),
        ],
        name="third_sum",
    )(in_vmem(got))

    grad, moved = pl.pallas_call(
        functools.partial(rows_kernel, nz=nz, half=half),
        in_specs=[vmem, vmem],
        out_specs=[vmem, vmem],
        out_shape=[jax.ShapeDtypeStruct((nz // 2, 2, half, width), jnp.bfloat16)] * 2,
        compiler_params=pltpu.CompilerParams(vmem_limit_bytes=VMEM_LIMIT),
        name="rows",
    )(in_vmem(pre), w_one)
    for i, step_by in enumerate((1, -1, 3)):
        moved = swapped(moved, "z", step_by)
        grad = grad.astype(jnp.float32) + moved.astype(jnp.float32)
        if i < 2:
            moved = grad[grad.shape[0] // 2 :].astype(jnp.bfloat16)
            grad = grad[: grad.shape[0] // 2]
    grad_feats = grad.astype(jnp.bfloat16)
    return (grad_feats, share_one, share_bias, share_two)


def solution(mesh):
    torus = Mesh(mesh.devices.reshape(4, 2, 2, 4, 8), ("yl", "co", "yh", "x", "z"))
    in_specs = (P(SUB, None, BLK, None), P(SUB, None), P(), P(), P())
    out_specs = (P(SUB, None, BLK, None), P(BLK, None), P(BLK), P(BLK, None))
    return jax.shard_map(step, mesh=torus, in_specs=in_specs, out_specs=out_specs, check_vma=False)
```

```python
import functools

import jax
import jax.numpy as jnp
from jax import lax
from jax.experimental import pallas as pl
from jax.experimental.pallas import tpu as pltpu
from jax.sharding import Mesh
from jax.sharding import PartitionSpec as P

BLK = ("yh", "x", "z")
SUB = ("yl", "co")
temper = 0.2
epsilon = 1e-06
LANES = 128
VMEM_LIMIT = 24 * 2**20
HELD = (0, 1)
RETURN_ORDER = (0, 3, 7, 4, 1, 6, 2, 5)


def shifted(value, axis, by):
    count = lax.axis_size(axis)
    return lax.ppermute(value, axis, [((i + by) % count, i) for i in range(count)])


def in_vmem(value):
    return pltpu.with_memory_space_constraint(value, pltpu.VMEM)


def in_hbm(value):
    return pltpu.with_memory_space_constraint(value, pltpu.HBM)


def swapped(value, axis, step_by):
    count = lax.axis_size(axis)
    pairs = [(i, (i + step_by * (1 - 2 * (i % 2))) % count) for i in range(count)]
    return lax.ppermute(value, axis, pairs)


def dot_nn(a, b):
    return lax.dot_general(a, b, (((1,), (0,)), ((), ())), preferred_element_type=jnp.float32)


def dot_nt(a, b):
    return lax.dot_general(a, b, (((1,), (1,)), ((), ())), preferred_element_type=jnp.float32)


def dot_tn(a, b):
    return lax.dot_general(a, b, (((0,), (0,)), ((), ())), preferred_element_type=jnp.float32)


def pos_of(pos_ref, block):
    start = pl.multiple_of(block // 2 * LANES, LANES)
    pair = jnp.broadcast_to(pos_ref[:, pl.ds(start, LANES)], (8, LANES))
    return jnp.where(lax.rem(block, 2) == 1, pltpu.roll(pair, LANES // 2, 1), pair)


def tile_kernel(*refs, nz, nx, ny, half, width, negatives, order):
    groups = 6
    rows_ref = refs[0]
    col_refs = refs[1 : 1 + groups]
    w_one_ref, w_two_ref, b_one_ref, pos_ref = refs[1 + groups : 5 + groups]
    kept_out, sent_out, weights_out, x_s, cols_s, hid_s, gp_s, pre_s, cpos_s = refs[5 + groups :]
    my_z, my_x, my_y = lax.axis_index("z"), lax.axis_index("x"), lax.axis_index("yh")
    my_yx = my_y * nx + my_x
    count = len(order)
    at = 0
    for ref in col_refs:
        for i in range(ref.shape[0]):
            for v in range(2):
                cols_s[v, at * half : (at + 1) * half, :] = ref[i, v * half : (v + 1) * half, :]
            at += 1
    lane = lax.broadcasted_iota(jnp.int32, (1, count * half), 1)
    cid = lax.rem(lane, half)
    for j, (dy, dx) in enumerate(order):
        block = (lax.rem(my_y + dy, ny) * nx + lax.rem(my_x + dx, nx)) * nz + my_z
        cid = cid + jnp.where(lane // half == j, block * half, 0)
        cpos_s[:, j * half : (j + 1) * half] = pos_of(pos_ref, block)[:1, :half]
    cpos = cpos_s[...]
    w_one = w_one_ref[...]
    w_two = w_two_ref[...]
    per = 256 // half
    chunk = per * half
    bias = jnp.zeros((1, width), jnp.float32)
    diagonal = lax.broadcasted_iota(jnp.int32, (half, LANES), 0) == lax.broadcasted_iota(
        jnp.int32, (half, LANES), 1
    )
    turn = 1 - 2 * lax.rem(my_z, 2)
    held = [lax.rem(my_z + turn * d + nz, nz) for d in RETURN_ORDER]
    half_iota = lax.broadcasted_iota(jnp.int32, (half, 1), 0)
    for v in range(2):
        for k in range(nz // per):
            blocks = held[k * per : (k + 1) * per]
            x = jnp.concatenate([rows_ref[b, v] for b in blocks], axis=0)
            stack_at = slice((v * nz * half) + k * chunk, (v * nz * half) + (k + 1) * chunk)
            pre = dot_nn(x, w_one) + b_one_ref[...]
            grow = jnp.exp(jnp.minimum(pre, 0.0))
            above = pre > 0
            hidden = jnp.where(above, pre, grow - 1.0).astype(jnp.bfloat16)
            slope = jnp.where(above, 1.0, grow)
            projected = dot_nn(hidden, w_two)
            radius = jnp.sqrt(jnp.sum(projected * projected, axis=1, keepdims=True) + epsilon)
            unit = projected / radius
            sent = unit.astype(jnp.bfloat16)
            rid = jnp.concatenate([(my_yx * nz + b) * half + half_iota for b in blocks], axis=0)
            if v == 0:
                rpos = jnp.concatenate(
                    [
                        jnp.sum(
                            jnp.where(diagonal, pos_of(pos_ref, my_yx * nz + b)[:1], 0),
                            axis=1,
                            keepdims=True,
                        )
                        for b in blocks
                    ],
                    axis=0,
                )
            total = None
            for cv in range(2):
                col = cols_s[cv]
                scores = dot_nt(sent, col) / temper
                g = jax.nn.sigmoid(scores)
                base = g * (2.0 / negatives)
                if v == cv:
                    coef = jnp.where(rid == cid, 0.0, base)
                elif v == 0:
                    coef = jnp.where(rpos == cid, 2.0 * g - 2.0, base)
                else:
                    coef = jnp.where(rid == cpos, 2.0 * g - 2.0, base)
                part = dot_nn(coef.astype(jnp.bfloat16), col)
                total = part if total is None else total + part
            grad_unit = total / temper
            inner = jnp.sum(unit * grad_unit, axis=1, keepdims=True)
            grad_proj = ((grad_unit - unit * inner) / radius).astype(jnp.bfloat16)
            grad_pre = (dot_nt(grad_proj, w_two) * slope).astype(jnp.bfloat16)
            grad_rows = dot_nt(grad_pre, w_one).astype(jnp.bfloat16)
            bias = bias + jnp.sum(grad_pre.astype(jnp.float32), axis=0, keepdims=True)
            x_s[stack_at, :] = x
            hid_s[stack_at, :] = hidden
            gp_s[stack_at, :] = grad_proj
            pre_s[stack_at, :] = grad_pre
            for j in range(per):
                place = (kept_out, sent_out)[(k * per + j) * 2 // nz]
                place[(k * per + j) % (nz // 2), v] = grad_rows[j * half : (j + 1) * half]
    parts = (
        dot_tn(x_s[...], pre_s[...]).astype(jnp.bfloat16),
        dot_tn(hid_s[...], gp_s[...]).astype(jnp.bfloat16),
    )
    per_x = width // (ny * nx)
    rows_x = ny * per_x
    tiles = width // LANES
    tile_lane = lax.broadcasted_iota(jnp.int32, (8, LANES), 1)
    for c in range(2):
        for x in range(nx):
            piece = c * nx + x
            for t in range(tiles):
                for y in range(ny):
                    source = (y * nx + x) * per_x
                    target = t * rows_x + y * per_x
                    weights_out[piece, target : target + per_x, :] = parts[c][
                        source : source + per_x, t * LANES : (t + 1) * LANES
                    ]
            picked = []
            for y in range(ny):
                source = (y * nx + x) * per_x
                low = source // LANES * LANES
                part = jnp.broadcast_to(bias[:, low : low + LANES], (8, LANES))
                by = (y * per_x - source) % LANES
                picked.append(pltpu.roll(part, by, 1) if by else part)
            row = jnp.where(tile_lane < per_x, picked[0], picked[1])
            weights_out[piece, tiles * rows_x :, :] = row.astype(jnp.bfloat16)


def spread(own_ref, out_ref):
    for i in range(out_ref.shape[0]):
        out_ref[i] = own_ref[...]


def first_sum(got_ref, out_ref, *, tiles, per_block, receivers):
    total = got_ref[0].astype(jnp.float32)
    for i in range(1, got_ref.shape[0]):
        total = total + got_ref[i].astype(jnp.float32)
    rows_x = receivers * per_block
    nz = out_ref.shape[0]
    for r in range(receivers):
        picked = [
            total[t * rows_x + r * per_block : t * rows_x + (r + 1) * per_block]
            for t in range(tiles)
        ]
        picked.append(total[tiles * rows_x :])
        out_ref[r % nz, r // nz] = jnp.concatenate(picked, axis=0).astype(jnp.bfloat16)


def second_sum(got_ref, out_ref):
    total = got_ref[0].astype(jnp.float32)
    for i in range(1, got_ref.shape[0]):
        total = total + got_ref[i].astype(jnp.float32)
    total = total.astype(jnp.bfloat16)
    for i in range(out_ref.shape[0]):
        out_ref[i] = total


def third_sum(got_ref, one_ref, two_ref, bias_ref, *, tiles, per_block, nz, ny, scale):
    for c, ref in enumerate((one_ref, two_ref)):
        total = None
        for i in range(got_ref.shape[0]):
            if i // ny % 2 == c:
                part = got_ref[i].astype(jnp.float32)
                total = part if total is None else total + part
        total = total * scale
        for t in range(tiles):
            ref[:, t * LANES : (t + 1) * LANES] = total[t * per_block : (t + 1) * per_block]
        if c == 0:
            start = (lax.axis_index("yh") * nz + lax.axis_index("z")) * per_block
            last = jnp.broadcast_to(total[tiles * per_block : tiles * per_block + 1], (8, LANES))
            last = pltpu.roll(last, lax.rem(LANES - start, LANES), 1)
            bias_ref[...] = last[0, :per_block]


def step(feats, pos, w_one, b_one, w_two):
    half = feats.shape[2]
    width = feats.shape[3]
    nz, nx, ny = lax.axis_size("z"), lax.axis_size("x"), lax.axis_size("yh")
    subs = lax.axis_size(SUB)
    blocks = nz * nx * ny
    negatives = 2.0 * half * blocks - 2.0
    own = feats[0]
    vmem = pl.BlockSpec(memory_space=pltpu.VMEM)
    copies = pl.pallas_call(
        spread,
        in_specs=[vmem],
        out_specs=vmem,
        out_shape=jax.ShapeDtypeStruct((nz, *own.shape), own.dtype),
        name="spread",
    )(own)
    rows = lax.all_to_all(copies, "z", 0, 0, tiled=True)

    flat = own.reshape(2 * half, width)
    pre_act = dot_nn(flat, w_one) + b_one
    hidden = jax.nn.elu(pre_act).astype(jnp.bfloat16)
    projected = dot_nn(hidden, w_two)
    radius = jnp.sqrt(jnp.sum(projected * projected, axis=1, keepdims=True) + epsilon)
    sent = (projected / radius).astype(jnp.bfloat16)[None]

    across = shifted(sent, "yh", 1)
    own_far = shifted(sent, "x", 2)
    both = jnp.concatenate([sent, across], axis=0)
    both_next = shifted(both, "x", 1)
    both_last = shifted(both, "x", 3)
    across_far = shifted(across, "x", 2)
    cols = [sent, across, both_next, both_last, own_far, across_far]
    order = [(0, 0), (1, 0), (0, 1), (1, 1), (0, 3), (1, 3), (0, 2), (1, 2)]
    piece_rows = width // nx // 2 * 2 * (width // LANES) + 8
    placed = [in_hbm(c) if i in HELD else in_vmem(c) for i, c in enumerate(cols)]
    kept, sent_back, weights = pl.pallas_call(
        lambda *refs: tile_kernel(
            *refs, nz=nz, nx=nx, ny=ny, half=half, width=width, negatives=negatives, order=order
        ),
        in_specs=[vmem] * (len(cols) + 5),
        out_specs=[vmem, vmem, vmem],
        out_shape=[
            jax.ShapeDtypeStruct((nz // 2, 2, half, width), jnp.bfloat16),
            jax.ShapeDtypeStruct((nz // 2, 2, half, width), jnp.bfloat16),
            jax.ShapeDtypeStruct((2 * nx, piece_rows, LANES), jnp.bfloat16),
        ],
        scratch_shapes=[
            pltpu.VMEM((2 * nz * half, width), jnp.bfloat16),
            pltpu.VMEM((2, len(order) * half, width), jnp.bfloat16),
            pltpu.VMEM((2 * nz * half, width), jnp.bfloat16),
            pltpu.VMEM((2 * nz * half, width), jnp.bfloat16),
            pltpu.VMEM((2 * nz * half, width), jnp.bfloat16),
            pltpu.VMEM((1, len(order) * half), jnp.int32),
        ],
        compiler_params=pltpu.CompilerParams(vmem_limit_bytes=VMEM_LIMIT),
        name="tile",
    )(in_vmem(rows), *placed, in_vmem(w_one), in_vmem(w_two), b_one[None], pos)

    tiles = width // LANES
    per_block = width // blocks
    receivers = ny * nz
    short = tiles * per_block + 8
    got = lax.all_to_all(weights, ("co", "x"), 0, 0, tiled=True)
    got = pl.pallas_call(
        functools.partial(first_sum, tiles=tiles, per_block=per_block, receivers=receivers),
        in_specs=[vmem],
        out_specs=vmem,
        out_shape=jax.ShapeDtypeStruct((nz, ny, short, LANES), jnp.bfloat16),
        name="first_sum",
    )(in_vmem(got))
    got = lax.all_to_all(got, "z", 0, 0, tiled=True)
    got = pl.pallas_call(
        second_sum,
        in_specs=[vmem],
        out_specs=vmem,
        out_shape=jax.ShapeDtypeStruct((subs, ny, short, LANES), jnp.bfloat16),
        name="second_sum",
    )(in_vmem(got))
    got = got.reshape(subs * ny, short, LANES)
    got = lax.all_to_all(got, ("yl", "co", "yh"), 0, 0, tiled=True)
    share_one, share_two, share_bias = pl.pallas_call(
        functools.partial(
            third_sum,
            tiles=tiles,
            per_block=per_block,
            nz=nz,
            ny=ny,
            scale=1.0 / (2.0 * half * blocks * subs),
        ),
        in_specs=[vmem],
        out_specs=[vmem] * 3,
        out_shape=[
            jax.ShapeDtypeStruct((per_block, width), jnp.float32),
            jax.ShapeDtypeStruct((per_block, width), jnp.float32),
            jax.ShapeDtypeStruct((per_block,), jnp.float32),
        ],
        name="third_sum",
    )(in_vmem(got))

    grad = kept
    moved = sent_back
    for i, step_by in enumerate((1, -1, 3)):
        moved = swapped(moved, "z", step_by)
        grad = grad.astype(jnp.float32) + moved.astype(jnp.float32)
        if i < 2:
            moved = grad[grad.shape[0] // 2 :].astype(jnp.bfloat16)
            grad = grad[: grad.shape[0] // 2]
    grad_feats = grad.astype(jnp.bfloat16)
    return (grad_feats, share_one, share_bias, share_two)


def solution(mesh):
    torus = Mesh(mesh.devices.reshape(4, 2, 2, 4, 8), ("yl", "co", "yh", "x", "z"))
    in_specs = (P(SUB, None, BLK, None), P(SUB, None), P(), P(), P())
    out_specs = (P(SUB, None, BLK, None), P(BLK, None), P(BLK), P(BLK, None))
    return jax.shard_map(step, mesh=torus, in_specs=in_specs, out_specs=out_specs, check_vma=False)
```

```python
import functools

import jax
import jax.numpy as jnp
from jax import lax
from jax.experimental import pallas as pl
from jax.experimental.pallas import tpu as pltpu
from jax.sharding import Mesh
from jax.sharding import PartitionSpec as P

BLK = ("yh", "x", "z")
SUB = ("yl", "co")
temper = 0.2
epsilon = 1e-06
LANES = 128
VMEM_LIMIT = 24 * 2**20
HELD = (0, 1)
RETURN_ORDER = (0, 3, 7, 4, 1, 6, 2, 5)


def shifted(value, axis, by):
    count = lax.axis_size(axis)
    return lax.ppermute(value, axis, [((i + by) % count, i) for i in range(count)])


def in_vmem(value):
    return pltpu.with_memory_space_constraint(value, pltpu.VMEM)


def in_hbm(value):
    return pltpu.with_memory_space_constraint(value, pltpu.HBM)


def swapped(value, axis, step_by):
    count = lax.axis_size(axis)
    pairs = [(i, (i + step_by * (1 - 2 * (i % 2))) % count) for i in range(count)]
    return lax.ppermute(value, axis, pairs)


def dot_nn(a, b):
    return lax.dot_general(a, b, (((1,), (0,)), ((), ())), preferred_element_type=jnp.float32)


def dot_nt(a, b):
    return lax.dot_general(a, b, (((1,), (1,)), ((), ())), preferred_element_type=jnp.float32)


def dot_tn(a, b):
    return lax.dot_general(a, b, (((0,), (0,)), ((), ())), preferred_element_type=jnp.float32)


def pos_of(pos_ref, block):
    start = pl.multiple_of(block // 2 * LANES, LANES)
    pair = jnp.broadcast_to(pos_ref[:, pl.ds(start, LANES)], (8, LANES))
    return jnp.where(lax.rem(block, 2) == 1, pltpu.roll(pair, LANES // 2, 1), pair)


def tile_kernel(*refs, nz, nx, ny, half, width, negatives, order):
    groups = 6
    rows_ref = refs[0]
    col_refs = refs[1 : 1 + groups]
    w_one_ref, w_two_ref, b_one_ref, pos_ref = refs[1 + groups : 5 + groups]
    kept_out, sent_out, weights_out, x_s, cols_s, hid_s, gp_s, pre_s, cpos_s, col_sem = refs[5 + groups :]
    my_z, my_x, my_y = lax.axis_index("z"), lax.axis_index("x"), lax.axis_index("yh")
    my_yx = my_y * nx + my_x
    count = len(order)
    early = [
        pltpu.make_async_copy(
            col_refs[i].at[0, pl.ds(v * half, half)],
            cols_s.at[v, pl.ds(i * half, half)],
            col_sem.at[2 * i + v],
        )
        for i in range(2)
        for v in range(2)
    ]
    for copy in early:
        copy.start()
    at = 2
    for ref in col_refs[2:]:
        for i in range(ref.shape[0]):
            for v in range(2):
                cols_s[v, at * half : (at + 1) * half, :] = ref[i, v * half : (v + 1) * half, :]
            at += 1
    lane = lax.broadcasted_iota(jnp.int32, (1, count * half), 1)
    cid = lax.rem(lane, half)
    for j, (dy, dx) in enumerate(order):
        block = (lax.rem(my_y + dy, ny) * nx + lax.rem(my_x + dx, nx)) * nz + my_z
        cid = cid + jnp.where(lane // half == j, block * half, 0)
        cpos_s[:, j * half : (j + 1) * half] = pos_of(pos_ref, block)[:1, :half]
    cpos = cpos_s[...]
    w_one = w_one_ref[...]
    w_two = w_two_ref[...]
    per = 256 // half
    chunk = per * half
    bias = jnp.zeros((1, width), jnp.float32)
    diagonal = lax.broadcasted_iota(jnp.int32, (half, LANES), 0) == lax.broadcasted_iota(
        jnp.int32, (half, LANES), 1
    )
    turn = 1 - 2 * lax.rem(my_z, 2)
    held = [lax.rem(my_z + turn * d + nz, nz) for d in RETURN_ORDER]
    half_iota = lax.broadcasted_iota(jnp.int32, (half, 1), 0)
    for v in range(2):
        for k in range(nz // per):
            blocks = held[k * per : (k + 1) * per]
            x = jnp.concatenate([rows_ref[b, v] for b in blocks], axis=0)
            stack_at = slice((v * nz * half) + k * chunk, (v * nz * half) + (k + 1) * chunk)
            pre = dot_nn(x, w_one) + b_one_ref[...]
            grow = jnp.exp(jnp.minimum(pre, 0.0))
            above = pre > 0
            hidden = jnp.where(above, pre, grow - 1.0).astype(jnp.bfloat16)
            slope = jnp.where(above, 1.0, grow)
            projected = dot_nn(hidden, w_two)
            radius = jnp.sqrt(jnp.sum(projected * projected, axis=1, keepdims=True) + epsilon)
            unit = projected / radius
            sent = unit.astype(jnp.bfloat16)
            rid = jnp.concatenate([(my_yx * nz + b) * half + half_iota for b in blocks], axis=0)
            if v == 0:
                rpos = jnp.concatenate(
                    [
                        jnp.sum(
                            jnp.where(diagonal, pos_of(pos_ref, my_yx * nz + b)[:1], 0),
                            axis=1,
                            keepdims=True,
                        )
                        for b in blocks
                    ],
                    axis=0,
                )
            if v == 0 and k == 0:
                for copy in early:
                    copy.wait()
            total = None
            for cv in range(2):
                col = cols_s[cv]
                scores = dot_nt(sent, col) / temper
                g = jax.nn.sigmoid(scores)
                base = g * (2.0 / negatives)
                if v == cv:
                    coef = jnp.where(rid == cid, 0.0, base)
                elif v == 0:
                    coef = jnp.where(rpos == cid, 2.0 * g - 2.0, base)
                else:
                    coef = jnp.where(rid == cpos, 2.0 * g - 2.0, base)
                part = dot_nn(coef.astype(jnp.bfloat16), col)
                total = part if total is None else total + part
            grad_unit = total / temper
            inner = jnp.sum(unit * grad_unit, axis=1, keepdims=True)
            grad_proj = ((grad_unit - unit * inner) / radius).astype(jnp.bfloat16)
            grad_pre = (dot_nt(grad_proj, w_two) * slope).astype(jnp.bfloat16)
            grad_rows = dot_nt(grad_pre, w_one).astype(jnp.bfloat16)
            bias = bias + jnp.sum(grad_pre.astype(jnp.float32), axis=0, keepdims=True)
            x_s[stack_at, :] = x
            hid_s[stack_at, :] = hidden
            gp_s[stack_at, :] = grad_proj
            pre_s[stack_at, :] = grad_pre
            for j in range(per):
                place = (kept_out, sent_out)[(k * per + j) * 2 // nz]
                place[(k * per + j) % (nz // 2), v] = grad_rows[j * half : (j + 1) * half]
    parts = (
        dot_tn(x_s[...], pre_s[...]).astype(jnp.bfloat16),
        dot_tn(hid_s[...], gp_s[...]).astype(jnp.bfloat16),
    )
    per_x = width // (ny * nx)
    rows_x = ny * per_x
    tiles = width // LANES
    tile_lane = lax.broadcasted_iota(jnp.int32, (8, LANES), 1)
    for c in range(2):
        for x in range(nx):
            piece = c * nx + x
            for t in range(tiles):
                for y in range(ny):
                    source = (y * nx + x) * per_x
                    target = t * rows_x + y * per_x
                    weights_out[piece, target : target + per_x, :] = parts[c][
                        source : source + per_x, t * LANES : (t + 1) * LANES
                    ]
            picked = []
            for y in range(ny):
                source = (y * nx + x) * per_x
                low = source // LANES * LANES
                part = jnp.broadcast_to(bias[:, low : low + LANES], (8, LANES))
                by = (y * per_x - source) % LANES
                picked.append(pltpu.roll(part, by, 1) if by else part)
            row = jnp.where(tile_lane < per_x, picked[0], picked[1])
            weights_out[piece, tiles * rows_x :, :] = row.astype(jnp.bfloat16)


def spread(own_ref, out_ref):
    for i in range(out_ref.shape[0]):
        out_ref[i] = own_ref[...]


def first_sum(got_ref, out_ref, *, tiles, per_block, receivers):
    total = got_ref[0].astype(jnp.float32)
    for i in range(1, got_ref.shape[0]):
        total = total + got_ref[i].astype(jnp.float32)
    rows_x = receivers * per_block
    for r in range(receivers):
        picked = [
            total[t * rows_x + r * per_block : t * rows_x + (r + 1) * per_block]
            for t in range(tiles)
        ]
        picked.append(total[tiles * rows_x :])
        out_ref[r] = jnp.concatenate(picked, axis=0).astype(jnp.bfloat16)


def second_sum(got_ref, out_ref):
    total = got_ref[0].astype(jnp.float32)
    for i in range(1, got_ref.shape[0]):
        total = total + got_ref[i].astype(jnp.float32)
    total = total.astype(jnp.bfloat16)
    for i in range(out_ref.shape[0]):
        out_ref[i] = total


def third_sum(got_ref, one_ref, two_ref, bias_ref, *, tiles, per_block, nz, scale):
    for c, ref in enumerate((one_ref, two_ref)):
        total = None
        for i in range(got_ref.shape[0]):
            if i % 2 == c:
                part = got_ref[i].astype(jnp.float32)
                total = part if total is None else total + part
        total = total * scale
        for t in range(tiles):
            ref[:, t * LANES : (t + 1) * LANES] = total[t * per_block : (t + 1) * per_block]
        if c == 0:
            start = (lax.axis_index("yh") * nz + lax.axis_index("z")) * per_block
            last = jnp.broadcast_to(total[tiles * per_block : tiles * per_block + 1], (8, LANES))
            last = pltpu.roll(last, lax.rem(LANES - start, LANES), 1)
            bias_ref[...] = last[0, :per_block]


def step(feats, pos, w_one, b_one, w_two):
    half = feats.shape[2]
    width = feats.shape[3]
    nz, nx, ny = lax.axis_size("z"), lax.axis_size("x"), lax.axis_size("yh")
    subs = lax.axis_size(SUB)
    blocks = nz * nx * ny
    negatives = 2.0 * half * blocks - 2.0
    own = feats[0]
    vmem = pl.BlockSpec(memory_space=pltpu.VMEM)
    copies = pl.pallas_call(
        spread,
        in_specs=[vmem],
        out_specs=vmem,
        out_shape=jax.ShapeDtypeStruct((nz, *own.shape), own.dtype),
        name="spread",
    )(own)
    rows = lax.all_to_all(copies, "z", 0, 0, tiled=True)

    flat = own.reshape(2 * half, width)
    pre_act = dot_nn(flat, w_one) + b_one
    hidden = jax.nn.elu(pre_act).astype(jnp.bfloat16)
    projected = dot_nn(hidden, w_two)
    radius = jnp.sqrt(jnp.sum(projected * projected, axis=1, keepdims=True) + epsilon)
    sent = (projected / radius).astype(jnp.bfloat16)[None]

    across = shifted(sent, "yh", 1)
    own_far = shifted(sent, "x", 2)
    both = jnp.concatenate([sent, across], axis=0)
    both_next = shifted(both, "x", 1)
    both_last = shifted(both, "x", 3)
    across_far = shifted(across, "x", 2)
    cols = [sent, across, both_next, both_last, own_far, across_far]
    order = [(0, 0), (1, 0), (0, 1), (1, 1), (0, 3), (1, 3), (0, 2), (1, 2)]
    piece_rows = width // nx // 2 * 2 * (width // LANES) + 8
    placed = [in_hbm(c) if i in HELD else in_vmem(c) for i, c in enumerate(cols)]
    kept, sent_back, weights = pl.pallas_call(
        lambda *refs: tile_kernel(
            *refs, nz=nz, nx=nx, ny=ny, half=half, width=width, negatives=negatives, order=order
        ),
        in_specs=[vmem] + [pl.BlockSpec(memory_space=pltpu.HBM)] * 2 + [vmem] * (len(cols) + 2),
        out_specs=[vmem, vmem, vmem],
        out_shape=[
            jax.ShapeDtypeStruct((nz // 2, 2, half, width), jnp.bfloat16),
            jax.ShapeDtypeStruct((nz // 2, 2, half, width), jnp.bfloat16),
            jax.ShapeDtypeStruct((2 * nx, piece_rows, LANES), jnp.bfloat16),
        ],
        scratch_shapes=[
            pltpu.VMEM((2 * nz * half, width), jnp.bfloat16),
            pltpu.VMEM((2, len(order) * half, width), jnp.bfloat16),
            pltpu.VMEM((2 * nz * half, width), jnp.bfloat16),
            pltpu.VMEM((2 * nz * half, width), jnp.bfloat16),
            pltpu.VMEM((2 * nz * half, width), jnp.bfloat16),
            pltpu.VMEM((1, len(order) * half), jnp.int32),
            pltpu.SemaphoreType.DMA((4,)),
        ],
        compiler_params=pltpu.CompilerParams(vmem_limit_bytes=VMEM_LIMIT),
        name="tile",
    )(in_vmem(rows), *placed, in_vmem(w_one), in_vmem(w_two), b_one[None], pos)

    tiles = width // LANES
    per_block = width // blocks
    receivers = ny * nz
    short = tiles * per_block + 8
    got = lax.all_to_all(weights, ("co", "x"), 0, 0, tiled=True)
    got = pl.pallas_call(
        functools.partial(first_sum, tiles=tiles, per_block=per_block, receivers=receivers),
        in_specs=[vmem],
        out_specs=vmem,
        out_shape=jax.ShapeDtypeStruct((receivers, short, LANES), jnp.bfloat16),
        name="first_sum",
    )(in_vmem(got))
    got = lax.all_to_all(got, ("yh", "z"), 0, 0, tiled=True)
    got = pl.pallas_call(
        second_sum,
        in_specs=[vmem],
        out_specs=vmem,
        out_shape=jax.ShapeDtypeStruct((subs, short, LANES), jnp.bfloat16),
        name="second_sum",
    )(in_vmem(got))
    got = lax.all_to_all(got, SUB, 0, 0, tiled=True)
    share_one, share_two, share_bias = pl.pallas_call(
        functools.partial(
            third_sum,
            tiles=tiles,
            per_block=per_block,
            nz=nz,
            scale=1.0 / (2.0 * half * blocks * subs),
        ),
        in_specs=[vmem],
        out_specs=[vmem] * 3,
        out_shape=[
            jax.ShapeDtypeStruct((per_block, width), jnp.float32),
            jax.ShapeDtypeStruct((per_block, width), jnp.float32),
            jax.ShapeDtypeStruct((per_block,), jnp.float32),
        ],
        name="third_sum",
    )(in_vmem(got))

    grad = kept
    moved = sent_back
    for i, step_by in enumerate((1, -1, 3)):
        moved = swapped(moved, "z", step_by)
        grad = grad.astype(jnp.float32) + moved.astype(jnp.float32)
        if i < 2:
            moved = grad[grad.shape[0] // 2 :].astype(jnp.bfloat16)
            grad = grad[: grad.shape[0] // 2]
    grad_feats = grad.astype(jnp.bfloat16)
    return (grad_feats, share_one, share_bias, share_two)


def solution(mesh):
    torus = Mesh(mesh.devices.reshape(4, 2, 2, 4, 8), ("yl", "co", "yh", "x", "z"))
    in_specs = (P(SUB, None, BLK, None), P(SUB, None), P(), P(), P())
    out_specs = (P(SUB, None, BLK, None), P(BLK, None), P(BLK), P(BLK, None))
    return jax.shard_map(step, mesh=torus, in_specs=in_specs, out_specs=out_specs, check_vma=False)
```

```python
import functools

import jax
import jax.numpy as jnp
from jax import lax
from jax.experimental import pallas as pl
from jax.experimental.pallas import tpu as pltpu
from jax.sharding import Mesh
from jax.sharding import PartitionSpec as P

BLK = ("yh", "x", "z")
SUB = ("yl", "co")
temper = 0.2
epsilon = 1e-06
LANES = 128
VMEM_LIMIT = 24 * 2**20
HELD = (0, 1)
RETURN_ORDER = (0, 3, 7, 4, 1, 6, 2, 5)


def shifted(value, axis, by):
    count = lax.axis_size(axis)
    return lax.ppermute(value, axis, [((i + by) % count, i) for i in range(count)])


def in_vmem(value):
    return pltpu.with_memory_space_constraint(value, pltpu.VMEM)


def in_hbm(value):
    return pltpu.with_memory_space_constraint(value, pltpu.HBM)


def swapped(value, axis, step_by):
    count = lax.axis_size(axis)
    pairs = [(i, (i + step_by * (1 - 2 * (i % 2))) % count) for i in range(count)]
    return lax.ppermute(value, axis, pairs)


def dot_nn(a, b):
    return lax.dot_general(a, b, (((1,), (0,)), ((), ())), preferred_element_type=jnp.float32)


def dot_nt(a, b):
    return lax.dot_general(a, b, (((1,), (1,)), ((), ())), preferred_element_type=jnp.float32)


def dot_tn(a, b):
    return lax.dot_general(a, b, (((0,), (0,)), ((), ())), preferred_element_type=jnp.float32)


def tile_kernel(*refs, nz, nx, ny, half, width, negatives, order):
    groups = 6
    rows_ref = refs[0]
    col_refs = refs[1 : 1 + groups]
    w_one_ref, w_two_ref, b_one_ref, pos_ref, pos_t_ref = refs[1 + groups : 6 + groups]
    kept_out, sent_out, weights_out, x_s, cols_s, hid_s, gp_s, pre_s, cpos_s = refs[6 + groups :]
    my_z, my_x, my_y = lax.axis_index("z"), lax.axis_index("x"), lax.axis_index("yh")
    my_yx = my_y * nx + my_x
    count = len(order)
    at = 0
    for ref in col_refs:
        for i in range(ref.shape[0]):
            for v in range(2):
                cols_s[v, at * half : (at + 1) * half, :] = ref[i, v * half : (v + 1) * half, :]
            at += 1
    lane = lax.broadcasted_iota(jnp.int32, (1, count * half), 1)
    cid = lax.rem(lane, half)
    for j, (dy, dx) in enumerate(order):
        block = (lax.rem(my_y + dy, ny) * nx + lax.rem(my_x + dx, nx)) * nz + my_z
        cid = cid + jnp.where(lane // half == j, block * half, 0)
        cpos_s[:, j * half : (j + 1) * half] = pos_ref[pl.ds(block, 1), :]
    cpos = cpos_s[...]
    w_one = w_one_ref[...]
    w_two = w_two_ref[...]
    per = 256 // half
    chunk = per * half
    bias = jnp.zeros((1, width), jnp.float32)
    block_lane = lax.broadcasted_iota(jnp.int32, pos_t_ref.shape, 1)
    turn = 1 - 2 * lax.rem(my_z, 2)
    held = [lax.rem(my_z + turn * d + nz, nz) for d in RETURN_ORDER]
    half_iota = lax.broadcasted_iota(jnp.int32, (half, 1), 0)
    for v in range(2):
        for k in range(nz // per):
            blocks = held[k * per : (k + 1) * per]
            x = jnp.concatenate([rows_ref[b, v] for b in blocks], axis=0)
            stack_at = slice((v * nz * half) + k * chunk, (v * nz * half) + (k + 1) * chunk)
            pre = dot_nn(x, w_one) + b_one_ref[...]
            grow = jnp.exp(jnp.minimum(pre, 0.0))
            above = pre > 0
            hidden = jnp.where(above, pre, grow - 1.0).astype(jnp.bfloat16)
            slope = jnp.where(above, 1.0, grow)
            projected = dot_nn(hidden, w_two)
            radius = jnp.sqrt(jnp.sum(projected * projected, axis=1, keepdims=True) + epsilon)
            unit = projected / radius
            sent = unit.astype(jnp.bfloat16)
            rid = jnp.concatenate([(my_yx * nz + b) * half + half_iota for b in blocks], axis=0)
            if v == 0:
                rpos = jnp.concatenate(
                    [
                        jnp.sum(
                            jnp.where(block_lane == my_yx * nz + b, pos_t_ref[...], 0),
                            axis=1,
                            keepdims=True,
                        )
                        for b in blocks
                    ],
                    axis=0,
                )
            total = None
            for cv in range(2):
                col = cols_s[cv]
                scores = dot_nt(sent, col) / temper
                g = jax.nn.sigmoid(scores)
                base = g * (2.0 / negatives)
                if v == cv:
                    coef = jnp.where(rid == cid, 0.0, base)
                elif v == 0:
                    coef = jnp.where(rpos == cid, 2.0 * g - 2.0, base)
                else:
                    coef = jnp.where(rid == cpos, 2.0 * g - 2.0, base)
                part = dot_nn(coef.astype(jnp.bfloat16), col)
                total = part if total is None else total + part
            grad_unit = total / temper
            inner = jnp.sum(unit * grad_unit, axis=1, keepdims=True)
            grad_proj = ((grad_unit - unit * inner) / radius).astype(jnp.bfloat16)
            grad_pre = (dot_nt(grad_proj, w_two) * slope).astype(jnp.bfloat16)
            grad_rows = dot_nt(grad_pre, w_one).astype(jnp.bfloat16)
            bias = bias + jnp.sum(grad_pre.astype(jnp.float32), axis=0, keepdims=True)
            x_s[stack_at, :] = x
            hid_s[stack_at, :] = hidden
            gp_s[stack_at, :] = grad_proj
            pre_s[stack_at, :] = grad_pre
            for j in range(per):
                place = (kept_out, sent_out)[(k * per + j) * 2 // nz]
                place[(k * per + j) % (nz // 2), v] = grad_rows[j * half : (j + 1) * half]
    parts = (
        dot_tn(x_s[...], pre_s[...]).astype(jnp.bfloat16),
        dot_tn(hid_s[...], gp_s[...]).astype(jnp.bfloat16),
    )
    per_x = width // (ny * nx)
    rows_x = ny * per_x
    tiles = width // LANES
    tile_lane = lax.broadcasted_iota(jnp.int32, (8, LANES), 1)
    for c in range(2):
        for x in range(nx):
            piece = c * nx + x
            for t in range(tiles):
                for y in range(ny):
                    source = (y * nx + x) * per_x
                    target = t * rows_x + y * per_x
                    weights_out[piece, target : target + per_x, :] = parts[c][
                        source : source + per_x, t * LANES : (t + 1) * LANES
                    ]
            picked = []
            for y in range(ny):
                source = (y * nx + x) * per_x
                low = source // LANES * LANES
                part = jnp.broadcast_to(bias[:, low : low + LANES], (8, LANES))
                by = (y * per_x - source) % LANES
                picked.append(pltpu.roll(part, by, 1) if by else part)
            row = jnp.where(tile_lane < per_x, picked[0], picked[1])
            weights_out[piece, tiles * rows_x :, :] = row.astype(jnp.bfloat16)


def spread(own_ref, out_ref):
    for i in range(out_ref.shape[0]):
        out_ref[i] = own_ref[...]


def first_sum(got_ref, out_ref, *, tiles, per_block, receivers):
    total = got_ref[0].astype(jnp.float32)
    for i in range(1, got_ref.shape[0]):
        total = total + got_ref[i].astype(jnp.float32)
    rows_x = receivers * per_block
    nz = out_ref.shape[0]
    for r in range(receivers):
        picked = [
            total[t * rows_x + r * per_block : t * rows_x + (r + 1) * per_block]
            for t in range(tiles)
        ]
        picked.append(total[tiles * rows_x :])
        out_ref[r % nz, r // nz] = jnp.concatenate(picked, axis=0).astype(jnp.bfloat16)


def second_sum(got_ref, out_ref):
    total = got_ref[0].astype(jnp.float32)
    for i in range(1, got_ref.shape[0]):
        total = total + got_ref[i].astype(jnp.float32)
    total = total.astype(jnp.bfloat16)
    for i in range(out_ref.shape[0]):
        out_ref[i] = total


def third_sum(got_ref, one_ref, two_ref, bias_ref, *, tiles, per_block, nz, ny, scale):
    for c, ref in enumerate((one_ref, two_ref)):
        total = None
        for i in range(got_ref.shape[0]):
            if i // ny % 2 == c:
                part = got_ref[i].astype(jnp.float32)
                total = part if total is None else total + part
        total = total * scale
        for t in range(tiles):
            ref[:, t * LANES : (t + 1) * LANES] = total[t * per_block : (t + 1) * per_block]
        if c == 0:
            start = (lax.axis_index("yh") * nz + lax.axis_index("z")) * per_block
            last = jnp.broadcast_to(total[tiles * per_block : tiles * per_block + 1], (8, LANES))
            last = pltpu.roll(last, lax.rem(LANES - start, LANES), 1)
            bias_ref[...] = last[0, :per_block]


def step(feats, pos, w_one, b_one, w_two):
    half = feats.shape[2]
    width = feats.shape[3]
    nz, nx, ny = lax.axis_size("z"), lax.axis_size("x"), lax.axis_size("yh")
    subs = lax.axis_size(SUB)
    blocks = nz * nx * ny
    negatives = 2.0 * half * blocks - 2.0
    own = feats[0]
    vmem = pl.BlockSpec(memory_space=pltpu.VMEM)
    copies = pl.pallas_call(
        spread,
        in_specs=[vmem],
        out_specs=vmem,
        out_shape=jax.ShapeDtypeStruct((nz, *own.shape), own.dtype),
        name="spread",
    )(own)
    rows = lax.all_to_all(copies, "z", 0, 0, tiled=True)

    flat = own.reshape(2 * half, width)
    pre_act = dot_nn(flat, w_one) + b_one
    hidden = jax.nn.elu(pre_act).astype(jnp.bfloat16)
    projected = dot_nn(hidden, w_two)
    radius = jnp.sqrt(jnp.sum(projected * projected, axis=1, keepdims=True) + epsilon)
    sent = (projected / radius).astype(jnp.bfloat16)[None]

    across = shifted(sent, "yh", 1)
    own_far = shifted(sent, "x", 2)
    both = jnp.concatenate([sent, across], axis=0)
    both_next = shifted(both, "x", 1)
    both_last = shifted(both, "x", 3)
    across_far = shifted(across, "x", 2)
    cols = [sent, across, both_next, both_last, own_far, across_far]
    order = [(0, 0), (1, 0), (0, 1), (1, 1), (0, 3), (1, 3), (0, 2), (1, 2)]
    piece_rows = width // nx // 2 * 2 * (width // LANES) + 8
    pos_square = pos[0].reshape(blocks, half)
    placed = [in_hbm(c) if i in HELD else in_vmem(c) for i, c in enumerate(cols)]
    kept, sent_back, weights = pl.pallas_call(
        lambda *refs: tile_kernel(
            *refs, nz=nz, nx=nx, ny=ny, half=half, width=width, negatives=negatives, order=order
        ),
        in_specs=[vmem] * (len(cols) + 6),
        out_specs=[vmem, vmem, vmem],
        out_shape=[
            jax.ShapeDtypeStruct((nz // 2, 2, half, width), jnp.bfloat16),
            jax.ShapeDtypeStruct((nz // 2, 2, half, width), jnp.bfloat16),
            jax.ShapeDtypeStruct((2 * nx, piece_rows, LANES), jnp.bfloat16),
        ],
        scratch_shapes=[
            pltpu.VMEM((2 * nz * half, width), jnp.bfloat16),
            pltpu.VMEM((2, len(order) * half, width), jnp.bfloat16),
            pltpu.VMEM((2 * nz * half, width), jnp.bfloat16),
            pltpu.VMEM((2 * nz * half, width), jnp.bfloat16),
            pltpu.VMEM((2 * nz * half, width), jnp.bfloat16),
            pltpu.VMEM((1, len(order) * half), jnp.int32),
        ],
        compiler_params=pltpu.CompilerParams(vmem_limit_bytes=VMEM_LIMIT),
        name="tile",
    )(in_vmem(rows), *placed, in_vmem(w_one), in_vmem(w_two), b_one[None], pos_square, pos_square.T)

    tiles = width // LANES
    per_block = width // blocks
    receivers = ny * nz
    short = tiles * per_block + 8
    got = lax.all_to_all(weights, ("co", "x"), 0, 0, tiled=True)
    got = pl.pallas_call(
        functools.partial(first_sum, tiles=tiles, per_block=per_block, receivers=receivers),
        in_specs=[vmem],
        out_specs=vmem,
        out_shape=jax.ShapeDtypeStruct((nz, ny, short, LANES), jnp.bfloat16),
        name="first_sum",
    )(in_vmem(got))
    got = lax.all_to_all(got, "z", 0, 0, tiled=True)
    got = pl.pallas_call(
        second_sum,
        in_specs=[vmem],
        out_specs=vmem,
        out_shape=jax.ShapeDtypeStruct((subs, ny, short, LANES), jnp.bfloat16),
        name="second_sum",
    )(in_vmem(got))
    got = got.reshape(subs * ny, short, LANES)
    got = lax.all_to_all(got, ("yl", "co", "yh"), 0, 0, tiled=True)
    share_one, share_two, share_bias = pl.pallas_call(
        functools.partial(
            third_sum,
            tiles=tiles,
            per_block=per_block,
            nz=nz,
            ny=ny,
            scale=1.0 / (2.0 * half * blocks * subs),
        ),
        in_specs=[vmem],
        out_specs=[vmem] * 3,
        out_shape=[
            jax.ShapeDtypeStruct((per_block, width), jnp.float32),
            jax.ShapeDtypeStruct((per_block, width), jnp.float32),
            jax.ShapeDtypeStruct((per_block,), jnp.float32),
        ],
        name="third_sum",
    )(in_vmem(got))

    grad = kept
    moved = sent_back
    for i, step_by in enumerate((1, -1, 3)):
        moved = swapped(moved, "z", step_by)
        grad = grad.astype(jnp.float32) + moved.astype(jnp.float32)
        if i < 2:
            moved = grad[grad.shape[0] // 2 :].astype(jnp.bfloat16)
            grad = grad[: grad.shape[0] // 2]
    grad_feats = grad.astype(jnp.bfloat16)
    return (grad_feats, share_one, share_bias, share_two)


def solution(mesh):
    torus = Mesh(mesh.devices.reshape(4, 2, 2, 4, 8), ("yl", "co", "yh", "x", "z"))
    in_specs = (P(SUB, None, BLK, None), P(SUB, None), P(), P(), P())
    out_specs = (P(SUB, None, BLK, None), P(BLK, None), P(BLK), P(BLK, None))
    return jax.shard_map(step, mesh=torus, in_specs=in_specs, out_specs=out_specs, check_vma=False)
```
